32 devices in a mesh: prompt: 2 (over x), head: 16 (over z, y, core).
Axes of the slice: x: 2, y: 2, z: 4, core: 2. Of those that a mesh axis runs over, the one named last changes fastest.
Arguments:
- queries: bfloat16 [8192, 128], P(('prompt', 'head')), may hold values from -1.5 to 1.5
- out_grad: bfloat16 [8192, 128], P(('prompt', 'head')), may hold values from -6 to 6
- row_route: int32 [8192, 1], P(('prompt', 'head')), may hold values from 0 to 63; in each aligned block of 256 rows (0 to 255, 256 to 511, ...) at most 8 rows name the same one
- row_live: int32 [8192], P(('prompt', 'head')), may hold values 0 or 1
- states: bfloat16 [2, 4128, 8192], P('prompt', None, 'head'), may hold values from -0.14941406 to 0.14941406
Outputs:
- query_grad: bfloat16 [8192, 128], P(('prompt', 'head'))
- state_grad: float32 [2, 4128, 8192], P('prompt', None, 'head')
The draws below stay inside these ranges and needn't reach their ends.
Inputs may be any that keep to these rules, and one draw needn't show every extreme that they name: `row_route`: among the 256 rows of one device no value appears more than 8 times, and some value appears exactly 8 times.
All inputs are finite; a program needn't handle non-finite values. No bound on the sum of `row_live` on one device may be relied on, other than what follows from the above.
Results may differ from the reference program's by a relative error of at most 0.0029.
Values may be sent and summed in bfloat16 or wider, within the bound.
No kernel may reach another device: no remote copies, remote signals or barrier semaphores. Data moves between devices by JAX's collectives and lax.ppermute only.
A program may use at most 128 MiB of HBM per device.

```python
import math
import jax
import jax.numpy as jnp
import numpy as np
from jax import lax

KVH = 32
HD = 128
FEAT = 8256
ROWS_DEV = 256
PROMPTS = 2
ROWS = 8192
CAP = 8
N_PROMPT = 2
N_HEAD = 16


def touch_ends(drawn, own_key, low, largest):
    longest = drawn.shape.index(max(drawn.shape))
    spots = []
    for shift in (0, 1):
        where = [jax.random.randint(jax.random.fold_in(own_key, axis), (), 0, length) for axis, length in enumerate(drawn.shape)]
        where[longest] = (where[longest] + shift) % drawn.shape[longest]
        spots.append(tuple(where))
    return drawn.at[spots[0]].set(low).at[spots[1]].set(largest)


def levels(rng, dims, shards, smallest, top_value):
    loudness, own = 1.0, jax.random.fold_in(rng, 6)
    for dim, parts in shards:
        draws = jnp.exp(jax.random.uniform(jax.random.fold_in(own, dim), (parts,), jnp.float32, smallest / len(shards), top_value / len(shards)))
        loudness = loudness * jnp.repeat(draws, dims[dim] // parts).reshape([-1 if axis == dim else 1 for axis in range(len(dims))])
    return loudness


def assign_block(own_key, own, number, rows, count, top, reach, lean):
    sequence = jax.random.permutation(own_key, count)
    packed, common = load_shares(count, rows * top, reach, lean, True), load_shares(count, rows * top, reach, lean, False)
    places = jnp.arange(count)

    def named(lengths, offset_by):
        used = int((lengths > 0).sum())
        fixed = max(1, used // 4)
        moved = fixed + (places - fixed + offset_by * (used - fixed)) % max(1, count - fixed)
        return jnp.zeros((count,), jnp.int32).at[sequence[jnp.where(places < fixed, places, moved)]].set(jnp.asarray(lengths, jnp.int32))

    lengths = jnp.where(number % 4 == 0, named(packed, number // 4), named(common, number - number // 4 - 1))
    mixed = jax.random.permutation(jax.random.fold_in(own, 3), count)
    donor, receiver = mixed[0:count // 2 * 2:2], mixed[1:count // 2 * 2:2]
    room = jnp.minimum(lengths[donor] - 1, reach - lengths[receiver]) // 2
    room = jnp.where((donor == sequence[0]) | (receiver == sequence[0]) | (lengths[receiver] == 0), 0, jnp.maximum(room, 0))
    moved = jax.random.randint(jax.random.fold_in(own, 4), (count // 2,), 0, 1 << 20) % (room + 1)
    lengths = lengths.at[donor].add(-moved).at[receiver].add(moved)
    items = jnp.searchsorted(jnp.cumsum(lengths), jnp.arange(rows * top), side="right").astype(jnp.int32)
    grid = items.reshape(top, rows).T
    grid = grid[jax.random.permutation(jax.random.fold_in(own, 1), rows)]
    offset_by = jax.random.randint(jax.random.fold_in(own, 2), (rows, 1), 0, top)
    return jnp.take_along_axis(grid, (jnp.arange(top)[None, :] + offset_by) % top, axis=1)


def load_shares(count, total, bound, lean, full):
    portions = [(1 << 20) // math.isqrt(rank ** lean) + 1 for rank in range(1, count + 1)]
    largest = bound if full else min(bound, max(-(-total // count), total * portions[0] // sum(portions)))
    least = 1 if total - largest >= count - 1 else 0
    holding, spare = [largest] + [least] * (count - 1), total - largest - least * (count - 1)
    while spare > 0:
        movable = [i for i in range(1, count) if holding[i] < largest] or [i for i in range(1, count) if holding[i] < bound]
        whole, left = sum([portions[i] for i in movable]), spare
        for i in movable:
            extra = min(bound - holding[i], max(1, left * portions[i] // whole), spare)
            holding[i] = holding[i] + extra
            spare = spare - extra
    return np.array(holding)


def scatter_about(own_key, shape, spread, bound, shards=(), kind=jnp.bfloat16):
    gain = levels(own_key, shape, shards, -0.22, 0.18) if shards else 1.0
    array = jax.random.normal(own_key, shape, jnp.float32) * spread * gain
    return jnp.minimum(jnp.maximum(array, -bound), bound).astype(kind)


def setup_inputs(seed: int = 0) -> dict:
    seeds = jax.random.split(jax.random.key(seed), 6)
    queries = scatter_about(seeds[0], (ROWS, HD), 0.25, 1.5, ((0, 32),))
    out_grad = scatter_about(seeds[1], (ROWS, HD), 1.0, 6.0, ((0, 32),))
    row_route_keys = jax.random.split(jax.random.fold_in(seeds[2], 1), ROWS // ROWS_DEV)
    row_route_turns = jax.random.permutation(jax.random.fold_in(seeds[2], 3), ROWS // ROWS_DEV)
    row_route = jax.vmap(lambda own, number: assign_block(jax.random.fold_in(seeds[2], 2), own, number, ROWS_DEV, PROMPTS * KVH, 1, CAP, 2))(row_route_keys, row_route_turns).reshape((ROWS, 1))
    row_live = touch_ends((jax.random.randint(seeds[3], (ROWS,), 0, 4) < 3).astype(jnp.int32), jax.random.fold_in(seeds[3], 1), 0, 1)
    states = scatter_about(seeds[4], (PROMPTS, FEAT // 2, 2 * KVH * HD), 0.025, 0.14941406, ((0, 2), (2, 16)))
    return dict(queries=queries, out_grad=out_grad, row_route=row_route, row_live=row_live, states=states)


def expand(query_float):
    head_dim = query_float.shape[-1]
    first_index, second_index = np.triu_indices(head_dim)
    coefficient = np.where(first_index == second_index, 1.0, np.sqrt(2.0)).astype(np.float32)
    return query_float[:, first_index] * query_float[:, second_index] * coefficient

def one_state(item):
    query_slots, grad_slots, state_block = item
    query_float = query_slots.astype(jnp.float32)
    features, pullback = jax.vjp(expand, query_float)
    stored = features.astype(jnp.bfloat16).astype(jnp.float32)
    grad_float = grad_slots.astype(jnp.float32)
    feature_grad = jnp.dot(grad_float, state_block.astype(jnp.float32).T, preferred_element_type=jnp.float32)
    query_part = pullback(feature_grad)[0]
    state_part = jnp.dot(stored.T, grad_float, preferred_element_type=jnp.float32)
    return (query_part, state_part)

def reference(queries, out_grad, row_route, row_live, states):
    sources = N_PROMPT * N_HEAD
    groups = PROMPTS * KVH
    slot_count = sources * CAP
    route_ids = row_route[:, 0].astype(jnp.int32)
    blocked = route_ids.reshape(sources, ROWS_DEV)
    one_hot = (blocked[:, :, None] == jnp.arange(groups, dtype=jnp.int32)[None, None, :]).astype(jnp.int32)
    running = jnp.cumsum(one_hot, axis=1)
    slot_rank = lax.optimization_barrier(jnp.sum(running * one_hot, axis=2)) - 1
    source_ids = jnp.arange(sources, dtype=jnp.int32)[:, None]
    slot_place = (blocked * slot_count + source_ids * CAP + slot_rank).reshape(-1).astype(jnp.int32)
    live_mask = row_live.astype(jnp.float32)[:, None]
    query_live = (queries.astype(jnp.float32) * live_mask).astype(queries.dtype)
    grad_live = (out_grad.astype(jnp.float32) * live_mask).astype(out_grad.dtype)
    query_slots = jnp.zeros((groups * slot_count, HD), queries.dtype).at[slot_place].set(query_live)
    grad_slots = jnp.zeros((groups * slot_count, HD), out_grad.dtype).at[slot_place].set(grad_live)
    query_slots = query_slots.reshape(groups, slot_count, HD)
    grad_slots = grad_slots.reshape(groups, slot_count, HD)
    full_states = states.reshape(PROMPTS, FEAT // 2, KVH * HD, 2).transpose(0, 1, 3, 2).reshape(PROMPTS, FEAT, KVH, HD)
    state_blocks = full_states.transpose(0, 2, 1, 3).reshape(groups, FEAT, HD)
    query_parts, state_parts = lax.map(one_state, (query_slots, grad_slots, state_blocks))
    query_grad = query_parts.reshape(groups * slot_count, HD)[slot_place].astype(jnp.bfloat16)
    full_grad = state_parts.reshape(PROMPTS, KVH, FEAT, HD).transpose(0, 2, 1, 3).reshape(PROMPTS, FEAT // 2, 2, KVH * HD)
    state_grad = full_grad.transpose(0, 1, 3, 2).reshape(PROMPTS, FEAT // 2, 2 * KVH * HD)
    return (query_grad, state_grad)
```

```python
import functools

import jax
import jax.numpy as jnp
import numpy as np
from jax import lax
from jax.experimental import pallas as pl
from jax.experimental.pallas import tpu as pltpu
from jax.sharding import PartitionSpec as P

KVH = 32


def score_grads(query_rows, grad_rows, sym_block, diag_block, mask_table):
    row_count, head_dim = query_rows.shape
    col_width = grad_rows.shape[1]
    block_rows = min(256, row_count)
    root_two = float(np.sqrt(2.0))
    query_blocks = query_rows.reshape(row_count // block_rows, block_rows, head_dim)
    grad_blocks = grad_rows.reshape(row_count // block_rows, block_rows, col_width)
    diag_float = diag_block.astype(jnp.float32)

    def block_step(total_grad, pair):
        query_block, grad_block = pair
        query_float = query_block.astype(jnp.float32)
        square = query_float[:, :, None] * query_float[:, None, :] * mask_table
        stored = square.reshape(block_rows, head_dim * head_dim).astype(jnp.bfloat16)
        total_grad = total_grad + lax.dot_general(
            stored, grad_block, (((0,), (0,)), ((), ())), preferred_element_type=jnp.float32
        )
        sweep = jnp.dot(query_block, sym_block, preferred_element_type=jnp.float32).reshape(
            block_rows, head_dim, col_width
        )
        sweep = (
            root_two * sweep
            - (2.0 * root_two - 2.0) * query_float[:, :, None] * diag_float[None, :, :]
        )
        grad_float = grad_block.astype(jnp.float32)
        query_part = jnp.einsum("baj,bj->ba", sweep, grad_float, precision=lax.Precision.HIGHEST)
        return (total_grad, query_part)

    start_grad = jnp.zeros((head_dim * head_dim, col_width), jnp.float32)
    total_grad, query_parts = lax.scan(block_step, start_grad, (query_blocks, grad_blocks))
    return (query_parts.reshape(row_count, head_dim), total_grad)


def general_device(queries, out_grad, row_route, row_live, states):
    prompt_count = lax.axis_size("prompt")
    head_count = lax.axis_size("head")
    rows_here, head_dim = queries.shape
    half_feat = states.shape[1]
    feat_count = 2 * half_feat
    column_count = states.shape[2] // 2
    kv_heads = KVH
    col_width = min(column_count, head_dim)
    copies = head_dim // col_width
    heads_held = column_count // col_width
    groups = prompt_count * kv_heads
    capacity = 2 * rows_here // groups
    first_index, second_index = np.triu_indices(head_dim)
    dense_place = (first_index * head_dim + second_index).astype(np.int32)
    triangle_of = np.full(head_dim * head_dim, feat_count, np.int32)
    triangle_of[dense_place] = np.arange(feat_count, dtype=np.int32)
    diagonal_of = triangle_of[np.arange(head_dim) * head_dim + np.arange(head_dim)]
    mask_np = np.zeros((head_dim, head_dim), np.float32)
    mask_np[first_index, second_index] = np.where(first_index == second_index, 1.0, np.sqrt(2.0))
    mask_table = jnp.asarray(mask_np)
    route_ids = row_route[:, 0]
    one_hot = (route_ids[:, None] == jnp.arange(groups, dtype=jnp.int32)[None, :]).astype(jnp.int32)
    slot_rank = jnp.sum(jnp.cumsum(one_hot, axis=0) * one_hot, axis=1) - 1
    slot_place = route_ids * capacity + slot_rank
    live_mask = row_live.astype(jnp.float32)[:, None]
    query_live = (queries.astype(jnp.float32) * live_mask).astype(jnp.bfloat16)
    grad_live = (out_grad.astype(jnp.float32) * live_mask).astype(jnp.bfloat16)
    query_bucket = (
        jnp.zeros((groups * capacity, head_dim), jnp.bfloat16).at[slot_place].set(query_live)
    )
    grad_bucket = (
        jnp.zeros((groups * capacity, head_dim), jnp.bfloat16).at[slot_place].set(grad_live)
    )
    query_send = jnp.broadcast_to(
        query_bucket.reshape(prompt_count, kv_heads, 1, capacity, head_dim),
        (prompt_count, kv_heads, copies, capacity, head_dim),
    )
    query_send = query_send.reshape(prompt_count, head_count, heads_held * capacity, head_dim)
    grad_send = grad_bucket.reshape(prompt_count, kv_heads, capacity, copies, col_width).transpose(
        0, 1, 3, 2, 4
    )
    grad_send = grad_send.reshape(prompt_count, head_count, heads_held * capacity, col_width)
    sectioned_query, sectioned_grad = (
        lax.all_to_all(query_send, "head", split_axis=1, concat_axis=1, tiled=True),
        lax.all_to_all(grad_send, "head", split_axis=1, concat_axis=1, tiled=True),
    )
    query_recv, grad_recv = (
        lax.all_to_all(sectioned_query, "prompt", split_axis=0, concat_axis=0, tiled=True),
        lax.all_to_all(sectioned_grad, "prompt", split_axis=0, concat_axis=0, tiled=True),
    )
    query_items = query_recv.reshape(prompt_count * head_count, heads_held, capacity, head_dim)
    grad_items = grad_recv.reshape(prompt_count * head_count, heads_held, capacity, col_width)
    local_state = (
        states[0]
        .reshape(half_feat, column_count, 2)
        .transpose(0, 2, 1)
        .reshape(feat_count, column_count)
    )
    padded_state = jnp.concatenate(
        [local_state, jnp.zeros((1, column_count), local_state.dtype)], axis=0
    )
    upper_state = padded_state[triangle_of].reshape(head_dim, head_dim, column_count)
    sym_state = upper_state + jnp.swapaxes(upper_state, 0, 1)
    diag_state = local_state[diagonal_of]
    query_shares = []
    state_shares = []
    for index in range(heads_held):
        query_rows = query_items[:, index].reshape(-1, head_dim)
        grad_rows = grad_items[:, index].reshape(-1, col_width)
        sym_block = sym_state[:, :, index * col_width : (index + 1) * col_width].reshape(
            head_dim, head_dim * col_width
        )
        diag_block = diag_state[:, index * col_width : (index + 1) * col_width]
        query_part, dense_grad = score_grads(
            query_rows, grad_rows, sym_block, diag_block, mask_table
        )
        query_shares.append(query_part.reshape(prompt_count * head_count, capacity, head_dim))
        state_shares.append(dense_grad[dense_place])
    query_partial = jnp.stack(query_shares, axis=1).reshape(
        prompt_count, head_count, heads_held * capacity, head_dim
    )
    state_full = jnp.concatenate(state_shares, axis=1)
    state_grad = (
        state_full.reshape(half_feat, 2, column_count)
        .transpose(0, 2, 1)
        .reshape(1, half_feat, 2 * column_count)
    )
    halfway = lax.all_to_all(query_partial, "head", split_axis=1, concat_axis=1, tiled=True)
    returned = lax.all_to_all(halfway, "prompt", split_axis=0, concat_axis=0, tiled=True)
    query_total = jnp.sum(
        returned.reshape(prompt_count, kv_heads, copies, capacity, head_dim), axis=2
    )
    query_grad = query_total.reshape(groups * capacity, head_dim)[slot_place].astype(jnp.bfloat16)
    return (query_grad, state_grad)


LANES = 128
SUB = 8


def pair_runs(head_dim):
    runs = []
    for a in range(head_dim):
        offset = a * head_dim - a * (a - 1) // 2
        for parity in range(2):
            b = a + (parity - offset) % 2
            if b < head_dim:
                first = (offset + b - a - parity) // 2
                runs.append((a, parity, b & 1, b >> 1, first, b == a))
    return runs


def split_place(index, head_dim):
    return (index & 1) * (head_dim // 2) + (index >> 1)


def eye_of(size, dtype=jnp.float32):
    return (
        lax.broadcasted_iota(jnp.int32, (size, size), 0)
        == lax.broadcasted_iota(jnp.int32, (size, size), 1)
    )


def parity_split(size):
    row = lax.broadcasted_iota(jnp.int32, (size, size), 0)
    col = lax.broadcasted_iota(jnp.int32, (size, size), 1)
    half = size // 2
    wanted = jnp.where(row < half, 2 * row, 2 * (row - half) + 1)
    return (col == wanted).astype(jnp.bfloat16)


def slot_row(route, rows, capacity):
    eye = eye_of(rows)
    wide = jnp.broadcast_to(route, (rows, rows))
    column = jnp.sum(jnp.where(eye, wide, 0), axis=1, keepdims=True)
    first = lax.broadcasted_iota(jnp.int32, (rows, rows), 0)
    second = lax.broadcasted_iota(jnp.int32, (rows, rows), 1)
    earlier = (column == wide) & (first < second)
    rank = jnp.sum(earlier.astype(jnp.int32), axis=0, keepdims=True)
    return route * capacity + rank


def pack_kernel(capacity, route_ref, live_ref, query_ref, grad_ref, send_ref):
    rows, head_dim = query_ref.shape
    slots = send_ref.shape[0]
    place = slot_row(route_ref[...], rows, capacity)
    place = jnp.where(live_ref[...] != 0, place, -1)
    pick = lax.broadcasted_iota(jnp.int32, (slots, rows), 0) == place
    pick = pick.astype(jnp.float32).astype(jnp.bfloat16)
    send_ref[:, :head_dim] = jnp.dot(
        pick, query_ref[...], preferred_element_type=jnp.float32
    ).astype(jnp.bfloat16)
    send_ref[:, head_dim:] = jnp.dot(
        pick, grad_ref[...], preferred_element_type=jnp.float32
    ).astype(jnp.bfloat16)


def unpack_kernel(capacity, route_ref, back_ref, out_ref):
    rows, head_dim = out_ref.shape
    slots = back_ref.shape[0]
    place = slot_row(route_ref[...], rows, capacity)
    eye = eye_of(rows)
    column = jnp.sum(
        jnp.where(eye, jnp.broadcast_to(place, (rows, rows)), 0), axis=1, keepdims=True
    )
    pick = lax.broadcasted_iota(jnp.int32, (rows, slots), 1) == column
    pick = pick.astype(jnp.float32).astype(jnp.bfloat16)
    out_ref[...] = jnp.dot(
        pick, back_ref[...], preferred_element_type=jnp.float32
    ).astype(jnp.bfloat16)


def head_rows(recv_ref, head, heads_held, capacity):
    slots, width = recv_ref.shape
    whole = recv_ref[...].astype(jnp.float32)
    split = whole.reshape(slots // (heads_held * capacity), heads_held, capacity, width)
    return split[:, head].reshape(slots // heads_held, width).astype(jnp.bfloat16)


def stuff_transposed(grad, parity):
    width = grad.shape[1]
    row = lax.broadcasted_iota(jnp.int32, (2 * width, width), 0)
    col = lax.broadcasted_iota(jnp.int32, (2 * width, width), 1)
    place = (row == 2 * col + parity).astype(jnp.bfloat16)
    return lax.dot_general(
        place, grad, (((1,), (1,)), ((), ())), preferred_element_type=jnp.float32
    ).astype(jnp.bfloat16)


def stuff(grad, parity):
    width = grad.shape[1]
    row = lax.broadcasted_iota(jnp.int32, (width, 2 * width), 0)
    col = lax.broadcasted_iota(jnp.int32, (width, 2 * width), 1)
    place = (col == 2 * row + parity).astype(jnp.bfloat16)
    return jnp.dot(grad, place, preferred_element_type=jnp.float32).astype(jnp.bfloat16)


def split_query(query):
    return lax.dot_general(
        parity_split(query.shape[1]),
        query,
        (((1,), (1,)), ((), ())),
        preferred_element_type=jnp.float32,
    )


def run_weight(start, diagonal, on_diagonal, off_diagonal):
    row = lax.broadcasted_iota(jnp.int32, (SUB, LANES), 0)
    value = jnp.where(row >= start, jnp.float32(off_diagonal), jnp.float32(0.0))
    if diagonal:
        value = jnp.where(row == start, jnp.float32(on_diagonal), value)
    return value


def query_kernel(
    heads_held, capacity, chunk, states_ref, recv_ref, out_ref,
    state_buf, xt_ref, feat_ref, acc_ref, dqt_ref, sem,
):
    half_feat, lanes = states_ref.shape
    slots, width = recv_ref.shape
    head_dim = width // 2
    half = head_dim // 2
    wide = lanes // heads_held
    rows = slots // heads_held
    cols = rows // LANES
    steps = half_feat // chunk
    copies = [
        pltpu.make_async_copy(
            states_ref.at[pl.ds(i * chunk, chunk)], state_buf.at[pl.ds(i * chunk, chunk)], sem.at[i]
        )
        for i in range(steps)
    ]
    for copy in copies:
        copy.start()
    stuffed = []
    for head in range(heads_held):
        block = head_rows(recv_ref, head, heads_held, capacity)
        grad = block[:, head_dim:]
        stuffed.append([stuff_transposed(grad, 0), stuff_transposed(grad, 1)])
        turned = split_query(block[:, :head_dim])
        for col in range(cols):
            xt_ref[head * cols + col] = turned[:, col * LANES : (col + 1) * LANES]
    for i in range(steps):
        copies[i].wait()
        for head in range(heads_held):
            part = state_buf[i * chunk : (i + 1) * chunk, head * wide : (head + 1) * wide]
            for parity in range(2):
                feat = jnp.dot(part, stuffed[head][parity], preferred_element_type=jnp.float32)
                for col in range(cols):
                    feat_ref[head * cols + col, parity, i * chunk : (i + 1) * chunk, :] = feat[
                        :, col * LANES : (col + 1) * LANES
                    ]
    runs = pair_runs(head_dim)
    regs = half // SUB
    inv_root = float(np.sqrt(0.5))

    def column(t, carry):
        values = [[xt_ref[t, p * half + m * SUB : p * half + (m + 1) * SUB, :] for m in range(regs)] for p in range(2)]
        totals = [[jnp.zeros((SUB, LANES), jnp.float32) for _ in range(regs)] for _ in range(2)]
        for a in range(head_dim):
            at = split_place(a, head_dim)
            own = jnp.broadcast_to(xt_ref[t, at : at + 1, :], (SUB, LANES))
            acc = None
            for owner, parity, side, start, first, diagonal in runs:
                if owner != a:
                    continue
                for m in range(start // SUB, regs):
                    place = first - start + m * SUB
                    feat = feat_ref[t, parity, place : place + SUB, :]
                    if m == start // SUB and (start % SUB or diagonal):
                        feat = feat * run_weight(start % SUB, diagonal, inv_root, 1.0)
                    term = feat * values[side][m]
                    acc = term if acc is None else acc + term
                    totals[side][m] = totals[side][m] + feat * own
            acc_ref[at * SUB : (at + 1) * SUB, :] = acc
        root = float(np.sqrt(2.0))
        for p in range(2):
            for m in range(regs):
                total = totals[p][m]
                base = (p * half + m * SUB) * SUB
                for k in range(SUB):
                    total = total + acc_ref[pl.ds(base + k, SUB, stride=SUB), :]
                dqt_ref[t, p * half + m * SUB : p * half + (m + 1) * SUB, :] = total * root
        return carry

    lax.fori_loop(0, heads_held * cols, column, 0)
    back = parity_split(head_dim)
    pieces = []
    for head in range(heads_held):
        turned = jnp.concatenate([dqt_ref[head * cols + col] for col in range(cols)], axis=1)
        part = lax.dot_general(
            turned.astype(jnp.bfloat16), back, (((0,), (0,)), ((), ())), preferred_element_type=jnp.float32
        )
        pieces.append(part.reshape(rows // capacity, 1, capacity, head_dim))
    out_ref[...] = jnp.concatenate(pieces, axis=1).reshape(slots, head_dim).astype(out_ref.dtype)


def state_kernel(
    heads_held, capacity, chunk, recv_ref, out_ref, xt_ref, feat_ref, stuffed_ref, out_buf, sem
):
    half_feat, lanes = out_ref.shape
    slots, width = recv_ref.shape
    head_dim = width // 2
    half = head_dim // 2
    wide = lanes // heads_held
    rows = slots // heads_held
    cols = rows // LANES
    steps = half_feat // chunk
    runs = pair_runs(head_dim)
    regs = half // SUB
    root = float(np.sqrt(2.0))
    for head in range(heads_held):
        block = head_rows(recv_ref, head, heads_held, capacity)
        grad = block[:, head_dim:]
        for parity in range(2):
            stuffed_ref[head, parity * rows : (parity + 1) * rows, :] = stuff(grad, parity)
        turned = split_query(block[:, :head_dim])
        for col in range(cols):
            xt_ref[head * cols + col] = turned[:, col * LANES : (col + 1) * LANES]

    def store_of(head, i):
        return pltpu.make_async_copy(
            out_buf.at[head, pl.ds(i * chunk, chunk)],
            out_ref.at[pl.ds(i * chunk, chunk), pl.ds(head * wide, wide)],
            sem.at[head, i],
        )

    for head in range(heads_held):

        def column(col, carry):
            t = head * cols + col
            values = [[xt_ref[t, p * half + m * SUB : p * half + (m + 1) * SUB, :] for m in range(regs)] for p in range(2)]
            for a, parity, side, start, first, diagonal in reversed(runs):
                at = split_place(a, head_dim)
                own = jnp.broadcast_to(xt_ref[t, at : at + 1, :], (SUB, LANES))
                for m in range(start // SUB, regs):
                    place = first - start + m * SUB
                    value = values[side][m] * own
                    if diagonal and m == start // SUB:
                        value = value * run_weight(start % SUB, True, 1.0, root)
                    else:
                        value = value * root
                    feat_ref[col, parity, place : place + SUB, :] = value
            return carry

        lax.fori_loop(0, cols, column, 0)

        def product(i, carry):
            at = pl.multiple_of(i * chunk, chunk)
            parts = [
                feat_ref[col, parity, pl.ds(at, chunk), :].astype(jnp.bfloat16)
                for parity in range(2)
                for col in range(cols)
            ]
            out_buf[head, pl.ds(at, chunk), :] = jnp.dot(
                jnp.concatenate(parts, axis=1), stuffed_ref[head], preferred_element_type=jnp.float32
            )
            store_of(head, i).start()
            return carry

        lax.fori_loop(0, steps, product, 0)

    def drain(i, carry):
        for head in range(heads_held):
            store_of(head, i).wait()
        return carry

    lax.fori_loop(0, steps, drain, 0)


def fast_device(queries, out_grad, row_route, row_live, states):
    axes = ("prompt", "head")
    prompt_count = lax.axis_size("prompt")
    rows_here, head_dim = queries.shape
    half_feat = states.shape[1]
    column_count = states.shape[2] // 2
    heads_held = column_count // head_dim
    groups = prompt_count * KVH
    capacity = 2 * rows_here // groups
    slots = groups * capacity
    chunk = half_feat // 6
    cols = slots // heads_held // LANES
    vmem = pl.BlockSpec(memory_space=pltpu.VMEM)
    hbm = pl.BlockSpec(memory_space=pl.ANY)
    params = pltpu.CompilerParams(vmem_limit_bytes=60 * 1024 * 1024)
    route = row_route.reshape(1, rows_here)
    live = row_live.reshape(1, rows_here)
    send = pl.pallas_call(
        functools.partial(pack_kernel, capacity),
        out_shape=jax.ShapeDtypeStruct((slots, 2 * head_dim), jnp.bfloat16),
        in_specs=[vmem] * 4,
        out_specs=vmem,
        name="pack_rows",
    )(route, live, queries, out_grad)
    recv = lax.all_to_all(send, axes, split_axis=0, concat_axis=0, tiled=True)
    answer = pl.pallas_call(
        functools.partial(query_kernel, heads_held, capacity, chunk),
        out_shape=jax.ShapeDtypeStruct((slots, head_dim), jnp.bfloat16),
        in_specs=[hbm, vmem],
        out_specs=vmem,
        scratch_shapes=[
            pltpu.VMEM((half_feat, 2 * column_count), jnp.bfloat16),
            pltpu.VMEM((heads_held * cols, head_dim, LANES), jnp.float32),
            pltpu.VMEM((heads_held * cols, 2, half_feat, LANES), jnp.float32),
            pltpu.VMEM((head_dim * SUB, LANES), jnp.float32),
            pltpu.VMEM((heads_held * cols, head_dim, LANES), jnp.float32),
            pltpu.SemaphoreType.DMA((half_feat // chunk,)),
        ],
        compiler_params=params,
        name="query_side",
    )(states[0], recv)
    back = lax.all_to_all(answer, axes, split_axis=0, concat_axis=0, tiled=True)
    state_grad = pl.pallas_call(
        functools.partial(state_kernel, heads_held, capacity, chunk),
        out_shape=jax.ShapeDtypeStruct((half_feat, 2 * column_count), jnp.float32),
        in_specs=[vmem],
        out_specs=hbm,
        scratch_shapes=[
            pltpu.VMEM((heads_held * cols, head_dim, LANES), jnp.float32),
            pltpu.VMEM((cols, 2, half_feat, LANES), jnp.float32),
            pltpu.VMEM((heads_held, 2 * slots // heads_held, 2 * head_dim), jnp.bfloat16),
            pltpu.VMEM((heads_held, half_feat, 2 * head_dim), jnp.float32),
            pltpu.SemaphoreType.DMA((heads_held, half_feat // chunk)),
        ],
        compiler_params=params,
        name="state_side",
    )(recv)
    query_grad = pl.pallas_call(
        functools.partial(unpack_kernel, capacity),
        out_shape=jax.ShapeDtypeStruct((rows_here, head_dim), jnp.bfloat16),
        in_specs=[vmem] * 2,
        out_specs=vmem,
        name="unpack_rows",
    )(route, back)
    return (query_grad, state_grad[None])


def whole_heads(queries, states):
    rows_here, head_dim = queries.shape
    groups = lax.axis_size("prompt") * KVH
    capacity = 2 * rows_here // groups
    column_count = states.shape[2] // 2
    heads_held = column_count // head_dim
    return (
        head_dim == LANES
        and heads_held >= 1
        and column_count % head_dim == 0
        and capacity % SUB == 0
        and (groups * capacity // heads_held) % LANES == 0
        and states.shape[1] % 96 == 0
    )


def per_device(*arrays):
    if whole_heads(arrays[0], arrays[4]):
        return fast_device(*arrays)
    return general_device(*arrays)


def solution(mesh):
    return jax.shard_map(
        per_device,
        mesh=mesh,
        in_specs=(
            P(("prompt", "head"), None),
            P(("prompt", "head"), None),
            P(("prompt", "head"), None),
            P(("prompt", "head")),
            P("prompt", None, "head"),
        ),
        out_specs=(P(("prompt", "head"), None), P("prompt", None, "head")),
        check_vma=False,
    )
```

```python
import functools

import jax
import jax.numpy as jnp
import numpy as np
from jax import lax
from jax.experimental import pallas as pl
from jax.experimental.pallas import tpu as pltpu
from jax.sharding import PartitionSpec as P

KVH = 32


def score_grads(query_rows, grad_rows, sym_block, diag_block, mask_table):
    row_count, head_dim = query_rows.shape
    col_width = grad_rows.shape[1]
    block_rows = min(256, row_count)
    root_two = float(np.sqrt(2.0))
    query_blocks = query_rows.reshape(row_count // block_rows, block_rows, head_dim)
    grad_blocks = grad_rows.reshape(row_count // block_rows, block_rows, col_width)
    diag_float = diag_block.astype(jnp.float32)

    def block_step(total_grad, pair):
        query_block, grad_block = pair
        query_float = query_block.astype(jnp.float32)
        square = query_float[:, :, None] * query_float[:, None, :] * mask_table
        stored = square.reshape(block_rows, head_dim * head_dim).astype(jnp.bfloat16)
        total_grad = total_grad + lax.dot_general(
            stored, grad_block, (((0,), (0,)), ((), ())), preferred_element_type=jnp.float32
        )
        sweep = jnp.dot(query_block, sym_block, preferred_element_type=jnp.float32).reshape(
            block_rows, head_dim, col_width
        )
        sweep = (
            root_two * sweep
            - (2.0 * root_two - 2.0) * query_float[:, :, None] * diag_float[None, :, :]
        )
        grad_float = grad_block.astype(jnp.float32)
        query_part = jnp.einsum("baj,bj->ba", sweep, grad_float, precision=lax.Precision.HIGHEST)
        return (total_grad, query_part)

    start_grad = jnp.zeros((head_dim * head_dim, col_width), jnp.float32)
    total_grad, query_parts = lax.scan(block_step, start_grad, (query_blocks, grad_blocks))
    return (query_parts.reshape(row_count, head_dim), total_grad)


def general_device(queries, out_grad, row_route, row_live, states):
    prompt_count = lax.axis_size("prompt")
    head_count = lax.axis_size("head")
    rows_here, head_dim = queries.shape
    half_feat = states.shape[1]
    feat_count = 2 * half_feat
    column_count = states.shape[2] // 2
    kv_heads = KVH
    col_width = min(column_count, head_dim)
    copies = head_dim // col_width
    heads_held = column_count // col_width
    groups = prompt_count * kv_heads
    capacity = 2 * rows_here // groups
    first_index, second_index = np.triu_indices(head_dim)
    dense_place = (first_index * head_dim + second_index).astype(np.int32)
    triangle_of = np.full(head_dim * head_dim, feat_count, np.int32)
    triangle_of[dense_place] = np.arange(feat_count, dtype=np.int32)
    diagonal_of = triangle_of[np.arange(head_dim) * head_dim + np.arange(head_dim)]
    mask_np = np.zeros((head_dim, head_dim), np.float32)
    mask_np[first_index, second_index] = np.where(first_index == second_index, 1.0, np.sqrt(2.0))
    mask_table = jnp.asarray(mask_np)
    route_ids = row_route[:, 0]
    one_hot = (route_ids[:, None] == jnp.arange(groups, dtype=jnp.int32)[None, :]).astype(jnp.int32)
    slot_rank = jnp.sum(jnp.cumsum(one_hot, axis=0) * one_hot, axis=1) - 1
    slot_place = route_ids * capacity + slot_rank
    live_mask = row_live.astype(jnp.float32)[:, None]
    query_live = (queries.astype(jnp.float32) * live_mask).astype(jnp.bfloat16)
    grad_live = (out_grad.astype(jnp.float32) * live_mask).astype(jnp.bfloat16)
    query_bucket = (
        jnp.zeros((groups * capacity, head_dim), jnp.bfloat16).at[slot_place].set(query_live)
    )
    grad_bucket = (
        jnp.zeros((groups * capacity, head_dim), jnp.bfloat16).at[slot_place].set(grad_live)
    )
    query_send = jnp.broadcast_to(
        query_bucket.reshape(prompt_count, kv_heads, 1, capacity, head_dim),
        (prompt_count, kv_heads, copies, capacity, head_dim),
    )
    query_send = query_send.reshape(prompt_count, head_count, heads_held * capacity, head_dim)
    grad_send = grad_bucket.reshape(prompt_count, kv_heads, capacity, copies, col_width).transpose(
        0, 1, 3, 2, 4
    )
    grad_send = grad_send.reshape(prompt_count, head_count, heads_held * capacity, col_width)
    sectioned_query, sectioned_grad = (
        lax.all_to_all(query_send, "head", split_axis=1, concat_axis=1, tiled=True),
        lax.all_to_all(grad_send, "head", split_axis=1, concat_axis=1, tiled=True),
    )
    query_recv, grad_recv = (
        lax.all_to_all(sectioned_query, "prompt", split_axis=0, concat_axis=0, tiled=True),
        lax.all_to_all(sectioned_grad, "prompt", split_axis=0, concat_axis=0, tiled=True),
    )
    query_items = query_recv.reshape(prompt_count * head_count, heads_held, capacity, head_dim)
    grad_items = grad_recv.reshape(prompt_count * head_count, heads_held, capacity, col_width)
    local_state = (
        states[0]
        .reshape(half_feat, column_count, 2)
        .transpose(0, 2, 1)
        .reshape(feat_count, column_count)
    )
    padded_state = jnp.concatenate(
        [local_state, jnp.zeros((1, column_count), local_state.dtype)], axis=0
    )
    upper_state = padded_state[triangle_of].reshape(head_dim, head_dim, column_count)
    sym_state = upper_state + jnp.swapaxes(upper_state, 0, 1)
    diag_state = local_state[diagonal_of]
    query_shares = []
    state_shares = []
    for index in range(heads_held):
        query_rows = query_items[:, index].reshape(-1, head_dim)
        grad_rows = grad_items[:, index].reshape(-1, col_width)
        sym_block = sym_state[:, :, index * col_width : (index + 1) * col_width].reshape(
            head_dim, head_dim * col_width
        )
        diag_block = diag_state[:, index * col_width : (index + 1) * col_width]
        query_part, dense_grad = score_grads(
            query_rows, grad_rows, sym_block, diag_block, mask_table
        )
        query_shares.append(query_part.reshape(prompt_count * head_count, capacity, head_dim))
        state_shares.append(dense_grad[dense_place])
    query_partial = jnp.stack(query_shares, axis=1).reshape(
        prompt_count, head_count, heads_held * capacity, head_dim
    )
    state_full = jnp.concatenate(state_shares, axis=1)
    state_grad = (
        state_full.reshape(half_feat, 2, column_count)
        .transpose(0, 2, 1)
        .reshape(1, half_feat, 2 * column_count)
    )
    halfway = lax.all_to_all(query_partial, "head", split_axis=1, concat_axis=1, tiled=True)
    returned = lax.all_to_all(halfway, "prompt", split_axis=0, concat_axis=0, tiled=True)
    query_total = jnp.sum(
        returned.reshape(prompt_count, kv_heads, copies, capacity, head_dim), axis=2
    )
    query_grad = query_total.reshape(groups * capacity, head_dim)[slot_place].astype(jnp.bfloat16)
    return (query_grad, state_grad)


LANES = 128
SUB = 8


def pair_runs(head_dim):
    runs = []
    for a in range(head_dim):
        offset = a * head_dim - a * (a - 1) // 2
        for parity in range(2):
            b = a + (parity - offset) % 2
            if b < head_dim:
                first = (offset + b - a - parity) // 2
                runs.append((a, parity, b & 1, b >> 1, first, b == a))
    return runs


def split_place(index, head_dim):
    return (index & 1) * (head_dim // 2) + (index >> 1)


def eye_of(size, dtype=jnp.float32):
    return (
        lax.broadcasted_iota(jnp.int32, (size, size), 0)
        == lax.broadcasted_iota(jnp.int32, (size, size), 1)
    )


def parity_split(size):
    row = lax.broadcasted_iota(jnp.int32, (size, size), 0)
    col = lax.broadcasted_iota(jnp.int32, (size, size), 1)
    half = size // 2
    wanted = jnp.where(row < half, 2 * row, 2 * (row - half) + 1)
    return (col == wanted).astype(jnp.bfloat16)


def slot_row(route, rows, capacity):
    eye = eye_of(rows)
    wide = jnp.broadcast_to(route, (rows, rows))
    column = jnp.sum(jnp.where(eye, wide, 0), axis=1, keepdims=True)
    first = lax.broadcasted_iota(jnp.int32, (rows, rows), 0)
    second = lax.broadcasted_iota(jnp.int32, (rows, rows), 1)
    earlier = (column == wide) & (first < second)
    rank = jnp.sum(earlier.astype(jnp.int32), axis=0, keepdims=True)
    return route * capacity + rank


def pack_kernel(
    capacity, route_hbm, live_hbm, query_hbm, grad_hbm, states_hbm,
    send_ref, held_ref, route_ref, live_ref, query_ref, grad_ref, sem,
):
    rows, head_dim = query_ref.shape
    slots = send_ref.shape[0]
    pairs = [
        (route_hbm, route_ref),
        (live_hbm, live_ref),
        (query_hbm, query_ref),
        (grad_hbm, grad_ref),
        (states_hbm, held_ref),
    ]
    copies = [pltpu.make_async_copy(*pair, sem.at[i]) for i, pair in enumerate(pairs)]
    for copy in copies:
        copy.start()
    copies[0].wait()
    copies[1].wait()
    place = slot_row(route_ref[...], rows, capacity)
    place = jnp.where(live_ref[...] != 0, place, -1)
    pick = lax.broadcasted_iota(jnp.int32, (slots, rows), 0) == place
    pick = pick.astype(jnp.float32).astype(jnp.bfloat16)
    copies[2].wait()
    send_ref[:, :head_dim] = jnp.dot(
        pick, query_ref[...], preferred_element_type=jnp.float32
    ).astype(jnp.bfloat16)
    copies[3].wait()
    send_ref[:, head_dim:] = jnp.dot(
        pick, grad_ref[...], preferred_element_type=jnp.float32
    ).astype(jnp.bfloat16)
    copies[4].wait()


def unpack_kernel(capacity, route_ref, back_ref, out_ref):
    rows, head_dim = out_ref.shape
    slots = back_ref.shape[0]
    place = slot_row(route_ref[...], rows, capacity)
    eye = eye_of(rows)
    column = jnp.sum(
        jnp.where(eye, jnp.broadcast_to(place, (rows, rows)), 0), axis=1, keepdims=True
    )
    pick = lax.broadcasted_iota(jnp.int32, (rows, slots), 1) == column
    pick = pick.astype(jnp.float32).astype(jnp.bfloat16)
    out_ref[...] = jnp.dot(
        pick, back_ref[...], preferred_element_type=jnp.float32
    ).astype(jnp.bfloat16)


def head_rows(recv_ref, head, heads_held, capacity):
    slots, width = recv_ref.shape
    whole = recv_ref[...].astype(jnp.float32)
    split = whole.reshape(slots // (heads_held * capacity), heads_held, capacity, width)
    return split[:, head].reshape(slots // heads_held, width).astype(jnp.bfloat16)


def stuff_transposed(grad, parity):
    width = grad.shape[1]
    row = lax.broadcasted_iota(jnp.int32, (2 * width, width), 0)
    col = lax.broadcasted_iota(jnp.int32, (2 * width, width), 1)
    place = (row == 2 * col + parity).astype(jnp.bfloat16)
    return lax.dot_general(
        place, grad, (((1,), (1,)), ((), ())), preferred_element_type=jnp.float32
    ).astype(jnp.bfloat16)


def stuff(grad, parity):
    width = grad.shape[1]
    row = lax.broadcasted_iota(jnp.int32, (width, 2 * width), 0)
    col = lax.broadcasted_iota(jnp.int32, (width, 2 * width), 1)
    place = (col == 2 * row + parity).astype(jnp.bfloat16)
    return jnp.dot(grad, place, preferred_element_type=jnp.float32).astype(jnp.bfloat16)


def split_query(query):
    return lax.dot_general(
        parity_split(query.shape[1]),
        query,
        (((1,), (1,)), ((), ())),
        preferred_element_type=jnp.float32,
    )


def run_weight(start, diagonal, on_diagonal, off_diagonal):
    row = lax.broadcasted_iota(jnp.int32, (SUB, LANES), 0)
    value = jnp.where(row >= start, jnp.float32(off_diagonal), jnp.float32(0.0))
    if diagonal:
        value = jnp.where(row == start, jnp.float32(on_diagonal), value)
    return value


def load_split(xt_ref, t, head_dim):
    half = head_dim // 2
    return [
        [xt_ref[t, at : at + SUB, :] for at in range(side * half, (side + 1) * half, SUB)]
        for side in range(2)
    ]


def prepare(recv_ref, xt_ref, heads_held, capacity):
    slots, width = recv_ref.shape
    head_dim = width // 2
    cols = slots // heads_held // LANES
    grads = []
    for head in range(heads_held):
        block = head_rows(recv_ref, head, heads_held, capacity)
        grads.append(block[:, head_dim:])
        turned = split_query(block[:, :head_dim])
        for col in range(cols):
            xt_ref[head * cols + col] = turned[:, col * LANES : (col + 1) * LANES]
    return grads


def query_kernel(
    heads_held, capacity, states_ref, recv_ref, out_ref,
    xt_ref, stuffed_ref, even_ref, odd_ref, acc_ref, total_ref, dqt_ref,
):
    half_feat, lanes = states_ref.shape
    slots, width = recv_ref.shape
    head_dim = width // 2
    half = head_dim // 2
    wide = lanes // heads_held
    rows = slots // heads_held
    cols = rows // LANES
    piece = half_feat // cols
    regs = half // SUB
    runs = pair_runs(head_dim)
    inv_root = float(np.sqrt(0.5))
    root = float(np.sqrt(2.0))
    feat_refs = [even_ref, odd_ref]
    grads = prepare(recv_ref, xt_ref, heads_held, capacity)
    for head in range(heads_held):
        for parity in range(2):
            stuffed_ref[2 * head + parity] = stuff_transposed(grads[head], parity)

    def expand(unit, col):
        head, parity = divmod(unit, 2)
        at = col * piece
        if not isinstance(col, int):
            at = pl.multiple_of(at, 2 * SUB)
        feat = jnp.dot(
            states_ref[pl.ds(at, piece), head * wide : (head + 1) * wide],
            stuffed_ref[unit],
            preferred_element_type=jnp.float32,
        )
        for other in range(cols):
            feat_refs[parity][other, pl.ds(at, piece), :] = feat[:, other * LANES : (other + 1) * LANES]

    def reduce(unit, col):
        head, parity = divmod(unit, 2)
        feat_ref = feat_refs[parity]
        t = head * cols + col
        values = load_split(xt_ref, t, head_dim)
        if parity == 0:
            totals = [[jnp.zeros((SUB, LANES), jnp.float32) for _ in range(regs)] for _ in range(2)]
        else:
            totals = load_split(total_ref, col, head_dim)
        for a, owner, side, start, first, diagonal in runs:
            if owner != parity:
                continue
            at = split_place(a, head_dim)
            own = jnp.broadcast_to(xt_ref[t, at : at + 1, :], (SUB, LANES))
            acc = None
            for m in range(start // SUB, regs):
                place = first - start + m * SUB
                feat = feat_ref[col, place : place + SUB, :]
                if m == start // SUB and (start % SUB or diagonal):
                    feat = feat * run_weight(start % SUB, diagonal, inv_root, 1.0)
                term = feat * values[side][m]
                acc = term if acc is None else acc + term
                totals[side][m] = totals[side][m] + feat * own
            acc_ref[col, parity, at * SUB : (at + 1) * SUB, :] = acc
        owners = {a for a, owner, *_ in runs if owner == parity}
        for a in sorted(set(range(head_dim)) - owners):
            at = split_place(a, head_dim)
            acc_ref[col, parity, at * SUB : (at + 1) * SUB, :] = jnp.zeros((SUB, LANES), jnp.float32)
        for side in range(2):
            for m in range(regs):
                at = side * half + m * SUB
                total = totals[side][m]
                if parity == 1:
                    for other in range(2):
                        for k in range(SUB):
                            total = total + acc_ref[col, other, pl.ds(at * SUB + k, SUB, stride=SUB), :]
                    dqt_ref[t, at : at + SUB, :] = total * root
                else:
                    total_ref[col, at : at + SUB, :] = total

    for col in range(cols):
        expand(0, col)
    units = 2 * heads_held
    for unit in range(units):

        def step(col, carry):
            if unit + 1 < units:
                expand(unit + 1, col)
            reduce(unit, col)
            return carry

        lax.fori_loop(0, cols, step, 0)
    back = parity_split(head_dim)
    pieces = []
    for head in range(heads_held):
        turned = jnp.concatenate([dqt_ref[head * cols + col] for col in range(cols)], axis=1)
        part = lax.dot_general(
            turned.astype(jnp.bfloat16), back, (((0,), (0,)), ((), ())), preferred_element_type=jnp.float32
        )
        pieces.append(part.reshape(rows // capacity, 1, capacity, head_dim))
    out_ref[...] = jnp.concatenate(pieces, axis=1).reshape(slots, head_dim).astype(out_ref.dtype)


def state_kernel(
    heads_held, capacity, recv_ref, out_ref, xt_ref, stuffed_ref, first_ref, second_ref, out_buf, sem
):
    half_feat, lanes = out_ref.shape
    slots, width = recv_ref.shape
    head_dim = width // 2
    wide = lanes // heads_held
    rows = slots // heads_held
    cols = rows // LANES
    piece = half_feat // cols
    runs = pair_runs(head_dim)
    regs = head_dim // 2 // SUB
    root = float(np.sqrt(2.0))
    feat_refs = [first_ref, second_ref]
    grads = prepare(recv_ref, xt_ref, heads_held, capacity)
    for head in range(heads_held):
        for parity in range(2):
            stuffed_ref[2 * head + parity] = stuff(grads[head], parity)

    def store_of(head, col):
        at = pl.multiple_of(col * piece, SUB)
        return pltpu.make_async_copy(
            out_buf.at[head, pl.ds(at, piece)],
            out_ref.at[pl.ds(at, piece), pl.ds(head * wide, wide)],
            sem.at[head, col],
        )

    def expand(head, col):
        feat_ref = feat_refs[head % 2]
        t = head * cols + col
        values = load_split(xt_ref, t, head_dim)
        for a, parity, side, start, first, diagonal in reversed(runs):
            at = split_place(a, head_dim)
            own = jnp.broadcast_to(xt_ref[t, at : at + 1, :], (SUB, LANES))
            for m in range(start // SUB, regs):
                place = first - start + m * SUB
                value = values[side][m] * own
                if diagonal and m == start // SUB:
                    value = value * run_weight(start % SUB, True, 1.0, root)
                else:
                    value = value * root
                feat_ref[col, parity, place : place + SUB, :] = value

    def product(head, col):
        feat_ref = feat_refs[head % 2]
        at = pl.multiple_of(col * piece, SUB)
        total = None
        for parity in range(2):
            part = jnp.concatenate(
                [feat_ref[other, parity, pl.ds(at, piece), :].astype(jnp.bfloat16) for other in range(cols)],
                axis=1,
            )
            term = jnp.dot(part, stuffed_ref[2 * head + parity], preferred_element_type=jnp.float32)
            total = term if total is None else total + term
        out_buf[head, pl.ds(at, piece), :] = total

    for head in range(heads_held + 1):

        def step(col, carry):
            if head > 0:
                product(head - 1, col)
            if head < heads_held:
                expand(head, col)
            if head > 0:
                store_of(head - 1, col).start()
            return carry

        lax.fori_loop(0, cols, step, 0)

    def drain(col, carry):
        for head in range(heads_held):
            store_of(head, col).wait()
        return carry

    lax.fori_loop(0, cols, drain, 0)


def fast_device(queries, out_grad, row_route, row_live, states):
    axes = ("prompt", "head")
    prompt_count = lax.axis_size("prompt")
    rows_here, head_dim = queries.shape
    half_feat = states.shape[1]
    column_count = states.shape[2] // 2
    heads_held = column_count // head_dim
    groups = prompt_count * KVH
    capacity = 2 * rows_here // groups
    slots = groups * capacity
    cols = slots // heads_held // LANES
    units = heads_held * cols
    vmem = pl.BlockSpec(memory_space=pltpu.VMEM)
    hbm = pl.BlockSpec(memory_space=pl.ANY)
    params = pltpu.CompilerParams(vmem_limit_bytes=48 * 1024 * 1024)
    route = row_route.reshape(1, rows_here)
    live = row_live.reshape(1, rows_here)
    send, held = pl.pallas_call(
        functools.partial(pack_kernel, capacity),
        out_shape=(
            pltpu.VMEM((slots, 2 * head_dim), jnp.bfloat16),
            pltpu.VMEM((half_feat, 2 * column_count), jnp.bfloat16),
        ),
        in_specs=[pl.BlockSpec(memory_space=pltpu.HBM)] * 5,
        out_specs=(vmem, vmem),
        scratch_shapes=[
            pltpu.VMEM((1, rows_here), jnp.int32),
            pltpu.VMEM((1, rows_here), jnp.int32),
            pltpu.VMEM((rows_here, head_dim), jnp.bfloat16),
            pltpu.VMEM((rows_here, head_dim), jnp.bfloat16),
            pltpu.SemaphoreType.DMA((5,)),
        ],
        compiler_params=pltpu.CompilerParams(vmem_limit_bytes=16 * 1024 * 1024),
        name="pack_rows",
    )(*[
        pltpu.with_memory_space_constraint(array, pltpu.HBM)
        for array in (route, live, queries, out_grad, states[0])
    ])
    recv = lax.all_to_all(send, axes, split_axis=0, concat_axis=0, tiled=True)
    recv = pltpu.with_memory_space_constraint(recv, pltpu.VMEM)
    answer = pl.pallas_call(
        functools.partial(query_kernel, heads_held, capacity),
        out_shape=jax.ShapeDtypeStruct((slots, head_dim), jnp.bfloat16),
        in_specs=[vmem, vmem],
        out_specs=vmem,
        scratch_shapes=[
            pltpu.VMEM((units, head_dim, LANES), jnp.float32),
            pltpu.VMEM((2 * heads_held, 2 * head_dim, slots // heads_held), jnp.bfloat16),
            pltpu.VMEM((cols, half_feat, LANES), jnp.float32),
            pltpu.VMEM((cols, half_feat, LANES), jnp.float32),
            pltpu.VMEM((cols, 2, head_dim * SUB, LANES), jnp.float32),
            pltpu.VMEM((cols, head_dim, LANES), jnp.float32),
            pltpu.VMEM((units, head_dim, LANES), jnp.float32),
        ],
        compiler_params=params,
        name="query_side",
    )(held, recv)
    back = lax.all_to_all(answer, axes, split_axis=0, concat_axis=0, tiled=True)
    back = pltpu.with_memory_space_constraint(back, pltpu.VMEM)
    state_grad = pl.pallas_call(
        functools.partial(state_kernel, heads_held, capacity),
        out_shape=jax.ShapeDtypeStruct((half_feat, 2 * column_count), jnp.float32),
        in_specs=[vmem],
        out_specs=hbm,
        scratch_shapes=[
            pltpu.VMEM((units, head_dim, LANES), jnp.float32),
            pltpu.VMEM((2 * heads_held, slots // heads_held, 2 * head_dim), jnp.bfloat16),
            pltpu.VMEM((cols, 2, half_feat, LANES), jnp.float32),
            pltpu.VMEM((cols, 2, half_feat, LANES), jnp.float32),
            pltpu.VMEM((heads_held, half_feat, 2 * head_dim), jnp.float32),
            pltpu.SemaphoreType.DMA((heads_held, cols)),
        ],
        compiler_params=params,
        name="state_side",
    )(recv)
    query_grad = pl.pallas_call(
        functools.partial(unpack_kernel, capacity),
        out_shape=jax.ShapeDtypeStruct((rows_here, head_dim), jnp.bfloat16),
        in_specs=[vmem] * 2,
        out_specs=vmem,
        name="unpack_rows",
    )(route, back)
    return (query_grad, state_grad[None])


def whole_heads(queries, states):
    rows_here, head_dim = queries.shape
    groups = lax.axis_size("prompt") * KVH
    capacity = 2 * rows_here // groups
    column_count = states.shape[2] // 2
    heads_held = column_count // head_dim
    return (
        head_dim == LANES
        and heads_held >= 1
        and column_count % head_dim == 0
        and capacity % SUB == 0
        and (groups * capacity // heads_held) % LANES == 0
        and states.shape[1] % (2 * SUB * (groups * capacity // heads_held // LANES)) == 0
    )


def per_device(*arrays):
    if whole_heads(arrays[0], arrays[4]):
        return fast_device(*arrays)
    return general_device(*arrays)


def solution(mesh):
    return jax.shard_map(
        per_device,
        mesh=mesh,
        in_specs=(
            P(("prompt", "head"), None),
            P(("prompt", "head"), None),
            P(("prompt", "head"), None),
            P(("prompt", "head")),
            P("prompt", None, "head"),
        ),
        out_specs=(P(("prompt", "head"), None), P("prompt", None, "head")),
        check_vma=False,
    )
```

```python
import functools

import jax
import jax.numpy as jnp
import numpy as np
from jax import lax
from jax.experimental import pallas as pl
from jax.experimental.pallas import tpu as pltpu
from jax.sharding import PartitionSpec as P

KVH = 32


def score_grads(query_rows, grad_rows, sym_block, diag_block, mask_table):
    row_count, head_dim = query_rows.shape
    col_width = grad_rows.shape[1]
    block_rows = min(256, row_count)
    root_two = float(np.sqrt(2.0))
    query_blocks = query_rows.reshape(row_count // block_rows, block_rows, head_dim)
    grad_blocks = grad_rows.reshape(row_count // block_rows, block_rows, col_width)
    diag_float = diag_block.astype(jnp.float32)

    def block_step(total_grad, pair):
        query_block, grad_block = pair
        query_float = query_block.astype(jnp.float32)
        square = query_float[:, :, None] * query_float[:, None, :] * mask_table
        stored = square.reshape(block_rows, head_dim * head_dim).astype(jnp.bfloat16)
        total_grad = total_grad + lax.dot_general(
            stored, grad_block, (((0,), (0,)), ((), ())), preferred_element_type=jnp.float32
        )
        sweep = jnp.dot(query_block, sym_block, preferred_element_type=jnp.float32).reshape(
            block_rows, head_dim, col_width
        )
        sweep = (
            root_two * sweep
            - (2.0 * root_two - 2.0) * query_float[:, :, None] * diag_float[None, :, :]
        )
        grad_float = grad_block.astype(jnp.float32)
        query_part = jnp.einsum("baj,bj->ba", sweep, grad_float, precision=lax.Precision.HIGHEST)
        return (total_grad, query_part)

    start_grad = jnp.zeros((head_dim * head_dim, col_width), jnp.float32)
    total_grad, query_parts = lax.scan(block_step, start_grad, (query_blocks, grad_blocks))
    return (query_parts.reshape(row_count, head_dim), total_grad)


def general_device(queries, out_grad, row_route, row_live, states):
    prompt_count = lax.axis_size("prompt")
    head_count = lax.axis_size("head")
    rows_here, head_dim = queries.shape
    half_feat = states.shape[1]
    feat_count = 2 * half_feat
    column_count = states.shape[2] // 2
    kv_heads = KVH
    col_width = min(column_count, head_dim)
    copies = head_dim // col_width
    heads_held = column_count // col_width
    groups = prompt_count * kv_heads
    capacity = 2 * rows_here // groups
    first_index, second_index = np.triu_indices(head_dim)
    dense_place = (first_index * head_dim + second_index).astype(np.int32)
    triangle_of = np.full(head_dim * head_dim, feat_count, np.int32)
    triangle_of[dense_place] = np.arange(feat_count, dtype=np.int32)
    diagonal_of = triangle_of[np.arange(head_dim) * head_dim + np.arange(head_dim)]
    mask_np = np.zeros((head_dim, head_dim), np.float32)
    mask_np[first_index, second_index] = np.where(first_index == second_index, 1.0, np.sqrt(2.0))
    mask_table = jnp.asarray(mask_np)
    route_ids = row_route[:, 0]
    one_hot = (route_ids[:, None] == jnp.arange(groups, dtype=jnp.int32)[None, :]).astype(jnp.int32)
    slot_rank = jnp.sum(jnp.cumsum(one_hot, axis=0) * one_hot, axis=1) - 1
    slot_place = route_ids * capacity + slot_rank
    live_mask = row_live.astype(jnp.float32)[:, None]
    query_live = (queries.astype(jnp.float32) * live_mask).astype(jnp.bfloat16)
    grad_live = (out_grad.astype(jnp.float32) * live_mask).astype(jnp.bfloat16)
    query_bucket = (
        jnp.zeros((groups * capacity, head_dim), jnp.bfloat16).at[slot_place].set(query_live)
    )
    grad_bucket = (
        jnp.zeros((groups * capacity, head_dim), jnp.bfloat16).at[slot_place].set(grad_live)
    )
    query_send = jnp.broadcast_to(
        query_bucket.reshape(prompt_count, kv_heads, 1, capacity, head_dim),
        (prompt_count, kv_heads, copies, capacity, head_dim),
    )
    query_send = query_send.reshape(prompt_count, head_count, heads_held * capacity, head_dim)
    grad_send = grad_bucket.reshape(prompt_count, kv_heads, capacity, copies, col_width).transpose(
        0, 1, 3, 2, 4
    )
    grad_send = grad_send.reshape(prompt_count, head_count, heads_held * capacity, col_width)
    sectioned_query, sectioned_grad = (
        lax.all_to_all(query_send, "head", split_axis=1, concat_axis=1, tiled=True),
        lax.all_to_all(grad_send, "head", split_axis=1, concat_axis=1, tiled=True),
    )
    query_recv, grad_recv = (
        lax.all_to_all(sectioned_query, "prompt", split_axis=0, concat_axis=0, tiled=True),
        lax.all_to_all(sectioned_grad, "prompt", split_axis=0, concat_axis=0, tiled=True),
    )
    query_items = query_recv.reshape(prompt_count * head_count, heads_held, capacity, head_dim)
    grad_items = grad_recv.reshape(prompt_count * head_count, heads_held, capacity, col_width)
    local_state = (
        states[0]
        .reshape(half_feat, column_count, 2)
        .transpose(0, 2, 1)
        .reshape(feat_count, column_count)
    )
    padded_state = jnp.concatenate(
        [local_state, jnp.zeros((1, column_count), local_state.dtype)], axis=0
    )
    upper_state = padded_state[triangle_of].reshape(head_dim, head_dim, column_count)
    sym_state = upper_state + jnp.swapaxes(upper_state, 0, 1)
    diag_state = local_state[diagonal_of]
    query_shares = []
    state_shares = []
    for index in range(heads_held):
        query_rows = query_items[:, index].reshape(-1, head_dim)
        grad_rows = grad_items[:, index].reshape(-1, col_width)
        sym_block = sym_state[:, :, index * col_width : (index + 1) * col_width].reshape(
            head_dim, head_dim * col_width
        )
        diag_block = diag_state[:, index * col_width : (index + 1) * col_width]
        query_part, dense_grad = score_grads(
            query_rows, grad_rows, sym_block, diag_block, mask_table
        )
        query_shares.append(query_part.reshape(prompt_count * head_count, capacity, head_dim))
        state_shares.append(dense_grad[dense_place])
    query_partial = jnp.stack(query_shares, axis=1).reshape(
        prompt_count, head_count, heads_held * capacity, head_dim
    )
    state_full = jnp.concatenate(state_shares, axis=1)
    state_grad = (
        state_full.reshape(half_feat, 2, column_count)
        .transpose(0, 2, 1)
        .reshape(1, half_feat, 2 * column_count)
    )
    halfway = lax.all_to_all(query_partial, "head", split_axis=1, concat_axis=1, tiled=True)
    returned = lax.all_to_all(halfway, "prompt", split_axis=0, concat_axis=0, tiled=True)
    query_total = jnp.sum(
        returned.reshape(prompt_count, kv_heads, copies, capacity, head_dim), axis=2
    )
    query_grad = query_total.reshape(groups * capacity, head_dim)[slot_place].astype(jnp.bfloat16)
    return (query_grad, state_grad)


LANES = 128
SUB = 8


def pair_runs(head_dim):
    runs = []
    for a in range(head_dim):
        offset = a * head_dim - a * (a - 1) // 2
        for parity in range(2):
            b = a + (parity - offset) % 2
            if b < head_dim:
                first = (offset + b - a - parity) // 2
                runs.append((a, parity, b & 1, b >> 1, first, b == a))
    return runs


def split_place(index, head_dim):
    return (index & 1) * (head_dim // 2) + (index >> 1)


def eye_of(size):
    return (
        lax.broadcasted_iota(jnp.int32, (size, size), 0)
        == lax.broadcasted_iota(jnp.int32, (size, size), 1)
    )


def parity_split(size):
    row = lax.broadcasted_iota(jnp.int32, (size, size), 0)
    col = lax.broadcasted_iota(jnp.int32, (size, size), 1)
    half = size // 2
    wanted = jnp.where(row < half, 2 * row, 2 * (row - half) + 1)
    return (col == wanted).astype(jnp.bfloat16)


def slot_row(route, groups, capacity):
    rows = route.shape[1]
    named = lax.broadcasted_iota(jnp.int32, (groups, rows), 0) == route
    named = named.astype(jnp.float32)
    first = lax.broadcasted_iota(jnp.int32, (rows, rows), 0)
    second = lax.broadcasted_iota(jnp.int32, (rows, rows), 1)
    earlier = (first < second).astype(jnp.float32).astype(jnp.bfloat16)
    before = jnp.dot(named.astype(jnp.bfloat16), earlier, preferred_element_type=jnp.float32)
    rank = jnp.sum(named * before, axis=0, keepdims=True)
    return route.astype(jnp.float32) * capacity + rank


def pack_kernel(
    capacity, route_hbm, live_hbm, query_hbm, grad_hbm, states_hbm,
    send_ref, held_ref, route_ref, live_ref, pair_ref, sem,
):
    rows, head_dim = query_hbm.shape
    slots = send_ref.shape[0]
    pairs = [
        (route_hbm, route_ref),
        (live_hbm, live_ref),
        (query_hbm, pair_ref.at[:, pl.ds(0, head_dim)]),
        (grad_hbm, pair_ref.at[:, pl.ds(head_dim, head_dim)]),
        (states_hbm.at[:, pl.ds(0, held_ref.shape[1])], held_ref),
    ]
    copies = [pltpu.make_async_copy(*pair, sem.at[i]) for i, pair in enumerate(pairs)]
    for copy in copies:
        copy.start()
    copies[0].wait()
    copies[1].wait()
    place = slot_row(route_ref[...], slots // capacity, capacity)
    place = jnp.where(live_ref[...] != 0, place.astype(jnp.int32), -1)
    pick = lax.broadcasted_iota(jnp.int32, (slots, rows), 0) == place
    pick = pick.astype(jnp.float32).astype(jnp.bfloat16)
    copies[2].wait()
    copies[3].wait()
    send_ref[...] = jnp.dot(
        pick, pair_ref[...], preferred_element_type=jnp.float32
    ).astype(jnp.bfloat16)
    copies[4].wait()


def unpack_kernel(pick_ref, back_ref, out_ref):
    out_ref[...] = jnp.dot(
        pick_ref[...], back_ref[...], preferred_element_type=jnp.float32
    ).astype(jnp.bfloat16)


def head_rows(recv_ref, head, heads_held, capacity):
    slots, width = recv_ref.shape
    whole = recv_ref[...].astype(jnp.float32)
    split = whole.reshape(slots // (heads_held * capacity), heads_held, capacity, width)
    return split[:, head].reshape(slots // heads_held, width).astype(jnp.bfloat16)


def stuff_transposed(grad, parity):
    width = grad.shape[1]
    row = lax.broadcasted_iota(jnp.int32, (2 * width, width), 0)
    col = lax.broadcasted_iota(jnp.int32, (2 * width, width), 1)
    place = (row == 2 * col + parity).astype(jnp.bfloat16)
    return lax.dot_general(
        place, grad, (((1,), (1,)), ((), ())), preferred_element_type=jnp.float32
    ).astype(jnp.bfloat16)


def stuff(grad, parity):
    width = grad.shape[1]
    row = lax.broadcasted_iota(jnp.int32, (width, 2 * width), 0)
    col = lax.broadcasted_iota(jnp.int32, (width, 2 * width), 1)
    place = (col == 2 * row + parity).astype(jnp.bfloat16)
    return jnp.dot(grad, place, preferred_element_type=jnp.float32).astype(jnp.bfloat16)


def split_query(query):
    return lax.dot_general(
        parity_split(query.shape[1]),
        query,
        (((1,), (1,)), ((), ())),
        preferred_element_type=jnp.float32,
    )


def run_weight(start, diagonal, on_diagonal, off_diagonal):
    row = lax.broadcasted_iota(jnp.int32, (SUB, LANES), 0)
    value = jnp.where(row >= start, jnp.float32(off_diagonal), jnp.float32(0.0))
    if diagonal:
        value = jnp.where(row == start, jnp.float32(on_diagonal), value)
    return value


def load_split(xt_ref, t, head_dim):
    half = head_dim // 2
    return [
        [xt_ref[t, at : at + SUB, :] for at in range(side * half, (side + 1) * half, SUB)]
        for side in range(2)
    ]


def prepare(recv_ref, xt_ref, heads_held, capacity):
    slots, width = recv_ref.shape
    head_dim = width // 2
    cols = slots // heads_held // LANES
    grads = []
    for head in range(heads_held):
        block = head_rows(recv_ref, head, heads_held, capacity)
        grads.append(block[:, head_dim:])
        turned = split_query(block[:, :head_dim])
        for col in range(cols):
            xt_ref[head * cols + col] = turned[:, col * LANES : (col + 1) * LANES]
    return grads


def query_kernel(
    heads_held, capacity, held_ref, recv_ref, states_hbm, out_ref,
    rest_ref, xt_ref, stuffed_ref, even_ref, odd_ref, acc_ref, dqt_ref, sem,
):
    half_feat, lanes = states_hbm.shape
    slots, width = recv_ref.shape
    head_dim = width // 2
    half = head_dim // 2
    wide = lanes // heads_held
    rows = slots // heads_held
    cols = rows // LANES
    piece = half_feat // cols
    regs = half // SUB
    runs = pair_runs(head_dim)
    inv_root = float(np.sqrt(0.5))
    root = float(np.sqrt(2.0))
    feat_refs = [even_ref, odd_ref]

    def fetch(head):
        return pltpu.make_async_copy(
            states_hbm.at[:, pl.ds(head * wide, wide)], rest_ref.at[head - 1], sem.at[head - 1]
        )

    for head in range(1, heads_held):
        fetch(head).start()
    grads = prepare(recv_ref, xt_ref, heads_held, capacity)
    for head in range(heads_held):
        for parity in range(2):
            stuffed_ref[2 * head + parity] = stuff_transposed(grads[head], parity)

    def expand(head, parity, start, stop):
        rows_of = pl.ds(start, stop - start)
        block = held_ref[rows_of] if head == 0 else rest_ref[head - 1, rows_of]
        feat = jnp.dot(block, stuffed_ref[2 * head + parity], preferred_element_type=jnp.float32)
        for col in range(cols):
            feat_refs[head % 2][parity, col, rows_of] = feat[:, col * LANES : (col + 1) * LANES]

    parts = 8
    tile = 2 * SUB
    bounds = [half_feat * i // parts // tile * tile for i in range(parts)] + [half_feat]
    lead = 1 * half_feat // parts

    def reduce(head, col, ahead):
        feat_ref = feat_refs[head % 2]
        t = head * cols + col
        values = load_split(xt_ref, t, head_dim)
        totals = [[None] * regs for _ in range(2)]
        fired = 0
        for a in range(head_dim):
            at = split_place(a, head_dim)
            own = jnp.broadcast_to(xt_ref[t, at : at + 1, :], (SUB, LANES))
            acc = None
            for owner, parity, side, start, first, diagonal in runs:
                if owner != a:
                    continue
                for m in range(start // SUB, regs):
                    place = first - start + m * SUB
                    while fired < parts and bounds[fired] < place + SUB + lead:
                        for unit in ahead:
                            expand(*unit, bounds[fired], bounds[fired + 1])
                        fired += 1
                    feat = feat_ref[parity, col, place : place + SUB, :]
                    if m == start // SUB and (start % SUB or diagonal):
                        feat = feat * run_weight(start % SUB, diagonal, inv_root, 1.0)
                    term = feat * values[side][m]
                    acc = term if acc is None else acc + term
                    other = feat * own
                    totals[side][m] = other if totals[side][m] is None else totals[side][m] + other
            acc_ref[col, at * SUB : (at + 1) * SUB, :] = acc
        for side in range(2):
            for m in range(regs):
                at = side * half + m * SUB
                total = totals[side][m]
                for k in range(SUB):
                    total = total + acc_ref[col, pl.ds(at * SUB + k, SUB, stride=SUB), :]
                dqt_ref[t, at : at + SUB, :] = total * root

    passes = []
    for head in range(heads_held):
        passes.append((head, 0, [(head, p) for p in range(2) if p == 1 or head == 0]))
        passes.append((head, 1, [(head + 1, 0)] if head + 1 < heads_held else []))

    def step(now, carry):
        for number, (head, col, ahead) in enumerate(passes):

            @pl.when(now == number)
            def _():
                if col == 1 and ahead:
                    fetch(head + 1).wait()
                reduce(head, col, ahead)

        return carry

    lax.fori_loop(0, len(passes), step, 0)
    back = parity_split(head_dim)
    pieces = []
    for head in range(heads_held):
        turned = jnp.concatenate([dqt_ref[head * cols + col] for col in range(cols)], axis=1)
        part = lax.dot_general(
            turned.astype(jnp.bfloat16), back, (((0,), (0,)), ((), ())), preferred_element_type=jnp.float32
        )
        pieces.append(part.reshape(rows // capacity, 1, capacity, head_dim))
    out_ref[...] = jnp.concatenate(pieces, axis=1).reshape(slots, head_dim).astype(out_ref.dtype)


def state_kernel(
    heads_held, capacity, recv_ref, route_ref, out_ref, pick_ref,
    xt_ref, stuffed_ref, first_ref, second_ref, out_buf, sem,
):
    half_feat, lanes = out_ref.shape
    slots, width = recv_ref.shape
    head_dim = width // 2
    wide = lanes // heads_held
    rows = slots // heads_held
    cols = rows // LANES
    piece = half_feat // cols
    runs = pair_runs(head_dim)
    regs = head_dim // 2 // SUB
    root = float(np.sqrt(2.0))
    feat_refs = [first_ref, second_ref]
    grads = prepare(recv_ref, xt_ref, heads_held, capacity)
    for head in range(heads_held):
        for parity in range(2):
            stuffed_ref[2 * head + parity] = stuff(grads[head], parity)

    def store_of(head, col):
        at = pl.multiple_of(col * piece, SUB)
        return pltpu.make_async_copy(
            out_buf.at[head, pl.ds(at, piece)],
            out_ref.at[pl.ds(at, piece), pl.ds(head * wide, wide)],
            sem.at[head, col],
        )

    def expand(head, col):
        feat_ref = feat_refs[head % 2]
        t = head * cols + col
        values = load_split(xt_ref, t, head_dim)
        for a, parity, side, start, first, diagonal in reversed(runs):
            at = split_place(a, head_dim)
            own = jnp.broadcast_to(xt_ref[t, at : at + 1, :], (SUB, LANES))
            for m in range(start // SUB, regs):
                place = first - start + m * SUB
                value = values[side][m] * own
                if diagonal and m == start // SUB:
                    value = value * run_weight(start % SUB, True, 1.0, root)
                else:
                    value = value * root
                feat_ref[col, parity, place : place + SUB, :] = value

    def product(head, col):
        feat_ref = feat_refs[head % 2]
        at = pl.multiple_of(col * piece, SUB)
        total = None
        for parity in range(2):
            part = jnp.concatenate(
                [feat_ref[other, parity, pl.ds(at, piece), :].astype(jnp.bfloat16) for other in range(cols)],
                axis=1,
            )
            term = jnp.dot(part, stuffed_ref[2 * head + parity], preferred_element_type=jnp.float32)
            total = term if total is None else total + term
        out_buf[head, pl.ds(at, piece), :] = total

    for head in range(heads_held + 1):

        def step(col, carry):
            if head > 0:
                product(head - 1, col)
            if head < heads_held:
                expand(head, col)
            if head > 0:
                store_of(head - 1, col).start()
            return carry

        lax.fori_loop(0, cols, step, 0)

    here = route_ref.shape[1]
    place = slot_row(route_ref[...], slots // capacity, capacity)
    column = jnp.sum(
        jnp.where(eye_of(here), jnp.broadcast_to(place, (here, here)), 0.0), axis=1, keepdims=True
    )
    pick = lax.broadcasted_iota(jnp.int32, (here, slots), 1) == column.astype(jnp.int32)
    pick_ref[...] = pick.astype(jnp.float32).astype(jnp.bfloat16)

    def drain(col, carry):
        for head in range(heads_held):
            store_of(head, col).wait()
        return carry

    lax.fori_loop(0, cols, drain, 0)


def fast_device(queries, out_grad, row_route, row_live, states):
    axes = ("prompt", "head")
    prompt_count = lax.axis_size("prompt")
    rows_here, head_dim = queries.shape
    half_feat = states.shape[1]
    column_count = states.shape[2] // 2
    heads_held = column_count // head_dim
    groups = prompt_count * KVH
    capacity = 2 * rows_here // groups
    slots = groups * capacity
    cols = slots // heads_held // LANES
    units = heads_held * cols
    vmem = pl.BlockSpec(memory_space=pltpu.VMEM)
    hbm = pl.BlockSpec(memory_space=pltpu.HBM)
    params = pltpu.CompilerParams(vmem_limit_bytes=48 * 1024 * 1024)
    route = row_route.reshape(1, rows_here)
    live = row_live.reshape(1, rows_here)
    inputs = [
        pltpu.with_memory_space_constraint(array, pltpu.HBM)
        for array in (route, live, queries, out_grad, states[0])
    ]
    send, held = pl.pallas_call(
        functools.partial(pack_kernel, capacity),
        out_shape=(
            pltpu.VMEM((slots, 2 * head_dim), jnp.bfloat16),
            pltpu.VMEM((half_feat, 2 * head_dim), jnp.bfloat16),
        ),
        in_specs=[hbm] * 5,
        out_specs=(vmem, vmem),
        scratch_shapes=[
            pltpu.VMEM((1, rows_here), jnp.int32),
            pltpu.VMEM((1, rows_here), jnp.int32),
            pltpu.VMEM((rows_here, 2 * head_dim), jnp.bfloat16),
            pltpu.SemaphoreType.DMA((5,)),
        ],
        compiler_params=pltpu.CompilerParams(vmem_limit_bytes=16 * 1024 * 1024),
        name="pack_rows",
    )(*inputs)
    recv = lax.all_to_all(send, axes, split_axis=0, concat_axis=0, tiled=True)
    recv = pltpu.with_memory_space_constraint(recv, pltpu.VMEM)
    answer = pl.pallas_call(
        functools.partial(query_kernel, heads_held, capacity),
        out_shape=jax.ShapeDtypeStruct((slots, head_dim), jnp.bfloat16),
        in_specs=[vmem, vmem, hbm],
        out_specs=vmem,
        scratch_shapes=[
            pltpu.VMEM((max(heads_held - 1, 1), half_feat, 2 * head_dim), jnp.bfloat16),
            pltpu.VMEM((units, head_dim, LANES), jnp.float32),
            pltpu.VMEM((2 * heads_held, 2 * head_dim, slots // heads_held), jnp.bfloat16),
            pltpu.VMEM((2, cols, half_feat, LANES), jnp.float32),
            pltpu.VMEM((2, cols, half_feat, LANES), jnp.float32),
            pltpu.VMEM((cols, head_dim * SUB, LANES), jnp.float32),
            pltpu.VMEM((units, head_dim, LANES), jnp.float32),
            pltpu.SemaphoreType.DMA((max(heads_held - 1, 1),)),
        ],
        compiler_params=params,
        name="query_side",
    )(held, recv, inputs[4])
    back = lax.all_to_all(answer, axes, split_axis=0, concat_axis=0, tiled=True)
    back = pltpu.with_memory_space_constraint(back, pltpu.VMEM)
    state_grad, pick = pl.pallas_call(
        functools.partial(state_kernel, heads_held, capacity),
        out_shape=(
            jax.ShapeDtypeStruct((half_feat, 2 * column_count), jnp.float32),
            pltpu.VMEM((rows_here, slots), jnp.bfloat16),
        ),
        in_specs=[vmem, vmem],
        out_specs=(hbm, vmem),
        scratch_shapes=[
            pltpu.VMEM((units, head_dim, LANES), jnp.float32),
            pltpu.VMEM((2 * heads_held, slots // heads_held, 2 * head_dim), jnp.bfloat16),
            pltpu.VMEM((cols, 2, half_feat, LANES), jnp.float32),
            pltpu.VMEM((cols, 2, half_feat, LANES), jnp.float32),
            pltpu.VMEM((heads_held, half_feat, 2 * head_dim), jnp.float32),
            pltpu.SemaphoreType.DMA((heads_held, cols)),
        ],
        compiler_params=params,
        name="state_side",
    )(recv, route)
    pick = pltpu.with_memory_space_constraint(pick, pltpu.VMEM)
    query_grad = pl.pallas_call(
        unpack_kernel,
        out_shape=jax.ShapeDtypeStruct((rows_here, head_dim), jnp.bfloat16),
        in_specs=[vmem] * 2,
        out_specs=vmem,
        name="unpack_rows",
    )(pick, back)
    return (query_grad, state_grad[None])


def whole_heads(queries, states):
    rows_here, head_dim = queries.shape
    groups = lax.axis_size("prompt") * KVH
    capacity = 2 * rows_here // groups
    column_count = states.shape[2] // 2
    heads_held = column_count // head_dim
    return (
        head_dim == LANES
        and heads_held >= 1
        and column_count % head_dim == 0
        and capacity % SUB == 0
        and groups * capacity // heads_held == 2 * LANES
        and states.shape[1] % (2 * SUB * (groups * capacity // heads_held // LANES)) == 0
    )


def per_device(*arrays):
    if whole_heads(arrays[0], arrays[4]):
        return fast_device(*arrays)
    return general_device(*arrays)


def solution(mesh):
    return jax.shard_map(
        per_device,
        mesh=mesh,
        in_specs=(
            P(("prompt", "head"), None),
            P(("prompt", "head"), None),
            P(("prompt", "head"), None),
            P(("prompt", "head")),
            P("prompt", None, "head"),
        ),
        out_specs=(P(("prompt", "head"), None), P("prompt", None, "head")),
        check_vma=False,
    )
```

```python
import functools

import jax
import jax.numpy as jnp
import numpy as np
from jax import lax
from jax.experimental import pallas as pl
from jax.experimental.pallas import tpu as pltpu
from jax.sharding import PartitionSpec as P

KVH = 32


def score_grads(query_rows, grad_rows, sym_block, diag_block, mask_table):
    row_count, head_dim = query_rows.shape
    col_width = grad_rows.shape[1]
    block_rows = min(256, row_count)
    root_two = float(np.sqrt(2.0))
    query_blocks = query_rows.reshape(row_count // block_rows, block_rows, head_dim)
    grad_blocks = grad_rows.reshape(row_count // block_rows, block_rows, col_width)
    diag_float = diag_block.astype(jnp.float32)

    def block_step(total_grad, pair):
        query_block, grad_block = pair
        query_float = query_block.astype(jnp.float32)
        square = query_float[:, :, None] * query_float[:, None, :] * mask_table
        stored = square.reshape(block_rows, head_dim * head_dim).astype(jnp.bfloat16)
        total_grad = total_grad + lax.dot_general(
            stored, grad_block, (((0,), (0,)), ((), ())), preferred_element_type=jnp.float32
        )
        sweep = jnp.dot(query_block, sym_block, preferred_element_type=jnp.float32).reshape(
            block_rows, head_dim, col_width
        )
        sweep = (
            root_two * sweep
            - (2.0 * root_two - 2.0) * query_float[:, :, None] * diag_float[None, :, :]
        )
        grad_float = grad_block.astype(jnp.float32)
        query_part = jnp.einsum("baj,bj->ba", sweep, grad_float, precision=lax.Precision.HIGHEST)
        return (total_grad, query_part)

    start_grad = jnp.zeros((head_dim * head_dim, col_width), jnp.float32)
    total_grad, query_parts = lax.scan(block_step, start_grad, (query_blocks, grad_blocks))
    return (query_parts.reshape(row_count, head_dim), total_grad)


def general_device(queries, out_grad, row_route, row_live, states):
    prompt_count = lax.axis_size("prompt")
    head_count = lax.axis_size("head")
    rows_here, head_dim = queries.shape
    half_feat = states.shape[1]
    feat_count = 2 * half_feat
    column_count = states.shape[2] // 2
    kv_heads = KVH
    col_width = min(column_count, head_dim)
    copies = head_dim // col_width
    heads_held = column_count // col_width
    groups = prompt_count * kv_heads
    capacity = 2 * rows_here // groups
    first_index, second_index = np.triu_indices(head_dim)
    dense_place = (first_index * head_dim + second_index).astype(np.int32)
    triangle_of = np.full(head_dim * head_dim, feat_count, np.int32)
    triangle_of[dense_place] = np.arange(feat_count, dtype=np.int32)
    diagonal_of = triangle_of[np.arange(head_dim) * head_dim + np.arange(head_dim)]
    mask_np = np.zeros((head_dim, head_dim), np.float32)
    mask_np[first_index, second_index] = np.where(first_index == second_index, 1.0, np.sqrt(2.0))
    mask_table = jnp.asarray(mask_np)
    route_ids = row_route[:, 0]
    one_hot = (route_ids[:, None] == jnp.arange(groups, dtype=jnp.int32)[None, :]).astype(jnp.int32)
    slot_rank = jnp.sum(jnp.cumsum(one_hot, axis=0) * one_hot, axis=1) - 1
    slot_place = route_ids * capacity + slot_rank
    live_mask = row_live.astype(jnp.float32)[:, None]
    query_live = (queries.astype(jnp.float32) * live_mask).astype(jnp.bfloat16)
    grad_live = (out_grad.astype(jnp.float32) * live_mask).astype(jnp.bfloat16)
    query_bucket = (
        jnp.zeros((groups * capacity, head_dim), jnp.bfloat16).at[slot_place].set(query_live)
    )
    grad_bucket = (
        jnp.zeros((groups * capacity, head_dim), jnp.bfloat16).at[slot_place].set(grad_live)
    )
    query_send = jnp.broadcast_to(
        query_bucket.reshape(prompt_count, kv_heads, 1, capacity, head_dim),
        (prompt_count, kv_heads, copies, capacity, head_dim),
    )
    query_send = query_send.reshape(prompt_count, head_count, heads_held * capacity, head_dim)
    grad_send = grad_bucket.reshape(prompt_count, kv_heads, capacity, copies, col_width).transpose(
        0, 1, 3, 2, 4
    )
    grad_send = grad_send.reshape(prompt_count, head_count, heads_held * capacity, col_width)
    sectioned_query, sectioned_grad = (
        lax.all_to_all(query_send, "head", split_axis=1, concat_axis=1, tiled=True),
        lax.all_to_all(grad_send, "head", split_axis=1, concat_axis=1, tiled=True),
    )
    query_recv, grad_recv = (
        lax.all_to_all(sectioned_query, "prompt", split_axis=0, concat_axis=0, tiled=True),
        lax.all_to_all(sectioned_grad, "prompt", split_axis=0, concat_axis=0, tiled=True),
    )
    query_items = query_recv.reshape(prompt_count * head_count, heads_held, capacity, head_dim)
    grad_items = grad_recv.reshape(prompt_count * head_count, heads_held, capacity, col_width)
    local_state = (
        states[0]
        .reshape(half_feat, column_count, 2)
        .transpose(0, 2, 1)
        .reshape(feat_count, column_count)
    )
    padded_state = jnp.concatenate(
        [local_state, jnp.zeros((1, column_count), local_state.dtype)], axis=0
    )
    upper_state = padded_state[triangle_of].reshape(head_dim, head_dim, column_count)
    sym_state = upper_state + jnp.swapaxes(upper_state, 0, 1)
    diag_state = local_state[diagonal_of]
    query_shares = []
    state_shares = []
    for index in range(heads_held):
        query_rows = query_items[:, index].reshape(-1, head_dim)
        grad_rows = grad_items[:, index].reshape(-1, col_width)
        sym_block = sym_state[:, :, index * col_width : (index + 1) * col_width].reshape(
            head_dim, head_dim * col_width
        )
        diag_block = diag_state[:, index * col_width : (index + 1) * col_width]
        query_part, dense_grad = score_grads(
            query_rows, grad_rows, sym_block, diag_block, mask_table
        )
        query_shares.append(query_part.reshape(prompt_count * head_count, capacity, head_dim))
        state_shares.append(dense_grad[dense_place])
    query_partial = jnp.stack(query_shares, axis=1).reshape(
        prompt_count, head_count, heads_held * capacity, head_dim
    )
    state_full = jnp.concatenate(state_shares, axis=1)
    state_grad = (
        state_full.reshape(half_feat, 2, column_count)
        .transpose(0, 2, 1)
        .reshape(1, half_feat, 2 * column_count)
    )
    halfway = lax.all_to_all(query_partial, "head", split_axis=1, concat_axis=1, tiled=True)
    returned = lax.all_to_all(halfway, "prompt", split_axis=0, concat_axis=0, tiled=True)
    query_total = jnp.sum(
        returned.reshape(prompt_count, kv_heads, copies, capacity, head_dim), axis=2
    )
    query_grad = query_total.reshape(groups * capacity, head_dim)[slot_place].astype(jnp.bfloat16)
    return (query_grad, state_grad)


LANES = 128
SUB = 8


def pair_runs(head_dim):
    runs = []
    for a in range(head_dim):
        offset = a * head_dim - a * (a - 1) // 2
        for parity in range(2):
            b = a + (parity - offset) % 2
            if b < head_dim:
                first = (offset + b - a - parity) // 2
                runs.append((a, parity, b & 1, b >> 1, first, b == a))
    return runs


def split_place(index, head_dim):
    return (index & 1) * (head_dim // 2) + (index >> 1)


def eye_of(size):
    return (
        lax.broadcasted_iota(jnp.int32, (size, size), 0)
        == lax.broadcasted_iota(jnp.int32, (size, size), 1)
    )


def parity_split(size):
    row = lax.broadcasted_iota(jnp.int32, (size, size), 0)
    col = lax.broadcasted_iota(jnp.int32, (size, size), 1)
    half = size // 2
    wanted = jnp.where(row < half, 2 * row, 2 * (row - half) + 1)
    return (col == wanted).astype(jnp.bfloat16)


def triangle(rows):
    first = lax.broadcasted_iota(jnp.int32, (rows, rows), 0)
    second = lax.broadcasted_iota(jnp.int32, (rows, rows), 1)
    return (first < second).astype(jnp.float32).astype(jnp.bfloat16)


def slot_row(route, earlier, groups, capacity):
    rows = route.shape[1]
    named = lax.broadcasted_iota(jnp.int32, (groups, rows), 0) == route
    named = named.astype(jnp.float32)
    before = jnp.dot(named.astype(jnp.bfloat16), earlier, preferred_element_type=jnp.float32)
    rank = jnp.sum(named * before, axis=0, keepdims=True)
    return route.astype(jnp.float32) * capacity + rank


def pack_kernel(
    capacity, route_hbm, live_hbm, query_hbm, grad_hbm, states_hbm,
    send_ref, held_ref, route_ref, live_ref, pair_ref, earlier_ref, sem,
):
    rows, head_dim = query_hbm.shape
    slots = send_ref.shape[0]
    pairs = [
        (route_hbm, route_ref),
        (live_hbm, live_ref),
        (query_hbm, pair_ref.at[:, pl.ds(0, head_dim)]),
        (grad_hbm, pair_ref.at[:, pl.ds(head_dim, head_dim)]),
        (states_hbm.at[pl.ds(0, held_ref.shape[0]), pl.ds(0, held_ref.shape[1])], held_ref),
    ]
    copies = [pltpu.make_async_copy(*pair, sem.at[i]) for i, pair in enumerate(pairs)]
    for copy in copies:
        copy.start()
    earlier_ref[...] = triangle(rows)
    copies[0].wait()
    copies[1].wait()
    place = slot_row(route_ref[...], earlier_ref[...], slots // capacity, capacity)
    place = jnp.where(live_ref[...] != 0, place.astype(jnp.int32), -1)
    pick = lax.broadcasted_iota(jnp.int32, (slots, rows), 0) == place
    pick = pick.astype(jnp.float32).astype(jnp.bfloat16)
    copies[2].wait()
    copies[3].wait()
    send_ref[...] = jnp.dot(
        pick, pair_ref[...], preferred_element_type=jnp.float32
    ).astype(jnp.bfloat16)
    copies[4].wait()


def unpack_kernel(pick_ref, back_ref, out_ref):
    out_ref[...] = jnp.dot(
        pick_ref[...], back_ref[...], preferred_element_type=jnp.float32
    ).astype(jnp.bfloat16)


def head_rows(recv_ref, head, heads_held, capacity):
    slots, width = recv_ref.shape
    whole = recv_ref[...].astype(jnp.float32)
    split = whole.reshape(slots // (heads_held * capacity), heads_held, capacity, width)
    return split[:, head].reshape(slots // heads_held, width).astype(jnp.bfloat16)


def stuff_transposed(grad, parity):
    width = grad.shape[1]
    row = lax.broadcasted_iota(jnp.int32, (2 * width, width), 0)
    col = lax.broadcasted_iota(jnp.int32, (2 * width, width), 1)
    place = (row == 2 * col + parity).astype(jnp.bfloat16)
    return lax.dot_general(
        place, grad, (((1,), (1,)), ((), ())), preferred_element_type=jnp.float32
    ).astype(jnp.bfloat16)


def stuff(grad, parity):
    width = grad.shape[1]
    row = lax.broadcasted_iota(jnp.int32, (width, 2 * width), 0)
    col = lax.broadcasted_iota(jnp.int32, (width, 2 * width), 1)
    place = (col == 2 * row + parity).astype(jnp.bfloat16)
    return jnp.dot(grad, place, preferred_element_type=jnp.float32).astype(jnp.bfloat16)


def split_query(query):
    return lax.dot_general(
        parity_split(query.shape[1]),
        query,
        (((1,), (1,)), ((), ())),
        preferred_element_type=jnp.float32,
    )


def run_weight(start, diagonal, on_diagonal, off_diagonal):
    row = lax.broadcasted_iota(jnp.int32, (SUB, LANES), 0)
    value = jnp.where(row >= start, jnp.float32(off_diagonal), jnp.float32(0.0))
    if diagonal:
        value = jnp.where(row == start, jnp.float32(on_diagonal), value)
    return value


def load_split(xt_ref, t, head_dim):
    half = head_dim // 2
    return [
        [xt_ref[t, at : at + SUB, :] for at in range(side * half, (side + 1) * half, SUB)]
        for side in range(2)
    ]


def prepare(recv_ref, xt_ref, heads_held, capacity):
    slots, width = recv_ref.shape
    head_dim = width // 2
    cols = slots // heads_held // LANES
    grads = []
    for head in range(heads_held):
        block = head_rows(recv_ref, head, heads_held, capacity)
        grads.append(block[:, head_dim:])
        turned = split_query(block[:, :head_dim])
        for col in range(cols):
            xt_ref[head * cols + col] = turned[:, col * LANES : (col + 1) * LANES]
    return grads


def query_kernel(
    heads_held, capacity, held_ref, recv_ref, states_hbm, out_ref,
    late_ref, rest_ref, xt_ref, stuffed_ref, even_ref, odd_ref, acc_ref, dqt_ref, sem,
):
    half_feat, lanes = states_hbm.shape
    early = held_ref.shape[0]
    slots, width = recv_ref.shape
    head_dim = width // 2
    half = head_dim // 2
    wide = lanes // heads_held
    rows = slots // heads_held
    cols = rows // LANES
    regs = half // SUB
    runs = pair_runs(head_dim)
    inv_root = float(np.sqrt(0.5))
    root = float(np.sqrt(2.0))
    feat_refs = [even_ref, odd_ref]

    def fetch(head):
        if head == 0:
            source, target = states_hbm.at[pl.ds(early, half_feat - early), pl.ds(0, wide)], late_ref
        else:
            source, target = states_hbm.at[:, pl.ds(head * wide, wide)], rest_ref.at[head - 1]
        return pltpu.make_async_copy(source, target, sem.at[head])

    for head in range(heads_held):
        fetch(head).start()
    grads = prepare(recv_ref, xt_ref, heads_held, capacity)
    for head in range(heads_held):
        for parity in range(2):
            stuffed_ref[2 * head + parity] = stuff_transposed(grads[head], parity)

    def expand(head, parity, start, stop):
        rows_of = pl.ds(start, stop - start)
        if head > 0:
            block = rest_ref[head - 1, rows_of]
        elif stop <= early:
            block = held_ref[rows_of]
        else:
            if start == early and parity == 0:
                fetch(0).wait()
            block = late_ref[start - early : stop - early]
        feat = jnp.dot(block, stuffed_ref[2 * head + parity], preferred_element_type=jnp.float32)
        for col in range(cols):
            feat_refs[head % 2][parity, col, rows_of] = feat[:, col * LANES : (col + 1) * LANES]

    parts = 2
    tile = 2 * SUB
    bounds = [half_feat * i // parts // tile * tile for i in range(parts)] + [half_feat]
    middle = next(a for a in range(head_dim) if a * head_dim - a * (a - 1) // 2 >= half_feat) - 1
    spans = [(0, middle), (middle, head_dim)]

    def reduce(head, col, part):
        low, high = spans[part]
        feat_ref = feat_refs[head % 2]
        t = head * cols + col
        values = load_split(xt_ref, t, head_dim)
        if part == 0:
            totals = [[None] * regs for _ in range(2)]
        else:
            totals = load_split(dqt_ref, t, head_dim)
        for a in range(low, high):
            at = split_place(a, head_dim)
            own = jnp.broadcast_to(xt_ref[t, at : at + 1, :], (SUB, LANES))
            acc = None
            for owner, parity, side, start, first, diagonal in runs:
                if owner != a:
                    continue
                for m in range(start // SUB, regs):
                    place = first - start + m * SUB
                    feat = feat_ref[parity, col, place : place + SUB, :]
                    if m == start // SUB and (start % SUB or diagonal):
                        feat = feat * run_weight(start % SUB, diagonal, inv_root, 1.0)
                    term = feat * values[side][m]
                    acc = term if acc is None else acc + term
                    other = feat * own
                    totals[side][m] = other if totals[side][m] is None else totals[side][m] + other
            acc_ref[col, at * SUB : (at + 1) * SUB, :] = acc
        for side in range(2):
            for m in range(regs):
                at = side * half + m * SUB
                total = totals[side][m]
                if part == 1:
                    for k in range(SUB):
                        total = total + acc_ref[col, pl.ds(at * SUB + k, SUB, stride=SUB), :]
                    total = total * root
                dqt_ref[t, at : at + SUB, :] = total

    regions = [([(0, 0)], [(0, 0, 0)]), ([(0, 1)], [(0, 1, 0), (0, 0, 1)])]
    for head in range(1, heads_held):
        regions.append(([(head, 0)], [(head - 1, 1, 1), (head, 0, 0)]))
        regions.append(([(head, 1)], [(head, 1, 0), (head, 0, 1)]))
    regions.append(([], [(heads_held - 1, 1, 1)]))

    def step(now, carry):
        for number, (ahead, segments) in enumerate(regions):

            @pl.when(now == number)
            def _():
                for head, group in ahead:
                    if head > 0 and group == 0:
                        fetch(head).wait()
                    for i in range(group * parts // 2, (group + 1) * parts // 2):
                        for parity in range(2):
                            expand(head, parity, bounds[i], bounds[i + 1])
                for head, col, part in segments:
                    reduce(head, col, part)

        return carry

    lax.fori_loop(0, len(regions), step, 0)
    back = parity_split(head_dim)
    pieces = []
    for head in range(heads_held):
        turned = jnp.concatenate([dqt_ref[head * cols + col] for col in range(cols)], axis=1)
        part = lax.dot_general(
            turned.astype(jnp.bfloat16), back, (((0,), (0,)), ((), ())), preferred_element_type=jnp.float32
        )
        pieces.append(part.reshape(rows // capacity, 1, capacity, head_dim))
    out_ref[...] = jnp.concatenate(pieces, axis=1).reshape(slots, head_dim).astype(out_ref.dtype)


def state_kernel(
    heads_held, capacity, recv_ref, route_ref, out_ref, pick_ref,
    xt_ref, stuffed_ref, first_ref, second_ref, out_buf, sem,
):
    half_feat, lanes = out_ref.shape
    slots, width = recv_ref.shape
    head_dim = width // 2
    wide = lanes // heads_held
    rows = slots // heads_held
    cols = rows // LANES
    piece = half_feat // cols
    runs = pair_runs(head_dim)
    regs = head_dim // 2 // SUB
    root = float(np.sqrt(2.0))
    feat_refs = [first_ref, second_ref]
    grads = prepare(recv_ref, xt_ref, heads_held, capacity)
    for head in range(heads_held):
        for parity in range(2):
            stuffed_ref[2 * head + parity] = stuff(grads[head], parity)

    def store_of(head, col):
        at = pl.multiple_of(col * piece, SUB)
        return pltpu.make_async_copy(
            out_buf.at[head, pl.ds(at, piece)],
            out_ref.at[pl.ds(at, piece), pl.ds(head * wide, wide)],
            sem.at[head, col],
        )

    def expand(head, col):
        feat_ref = feat_refs[head % 2]
        t = head * cols + col
        values = load_split(xt_ref, t, head_dim)
        for a, parity, side, start, first, diagonal in reversed(runs):
            at = split_place(a, head_dim)
            own = jnp.broadcast_to(xt_ref[t, at : at + 1, :], (SUB, LANES))
            for m in range(start // SUB, regs):
                place = first - start + m * SUB
                value = values[side][m] * own
                if diagonal and m == start // SUB:
                    value = value * run_weight(start % SUB, True, 1.0, root)
                else:
                    value = value * root
                feat_ref[col, parity, place : place + SUB, :] = value

    def product(head, col):
        feat_ref = feat_refs[head % 2]
        at = pl.multiple_of(col * piece, SUB)
        total = None
        for parity in range(2):
            part = jnp.concatenate(
                [feat_ref[other, parity, pl.ds(at, piece), :].astype(jnp.bfloat16) for other in range(cols)],
                axis=1,
            )
            term = jnp.dot(part, stuffed_ref[2 * head + parity], preferred_element_type=jnp.float32)
            total = term if total is None else total + term
        out_buf[head, pl.ds(at, piece), :] = total

    for head in range(heads_held + 1):

        def step(col, carry):
            if head > 0:
                product(head - 1, col)
            if head < heads_held:
                expand(head, col)
            if head > 0:
                store_of(head - 1, col).start()
            return carry

        lax.fori_loop(0, cols, step, 0)

    here = route_ref.shape[1]
    place = slot_row(route_ref[...], triangle(here), slots // capacity, capacity)
    column = jnp.sum(
        jnp.where(eye_of(here), jnp.broadcast_to(place, (here, here)), 0.0), axis=1, keepdims=True
    )
    pick = lax.broadcasted_iota(jnp.int32, (here, slots), 1) == column.astype(jnp.int32)
    pick_ref[...] = pick.astype(jnp.float32).astype(jnp.bfloat16)

    def drain(col, carry):
        for head in range(heads_held):
            store_of(head, col).wait()
        return carry

    lax.fori_loop(0, cols, drain, 0)


def fast_device(queries, out_grad, row_route, row_live, states):
    axes = ("prompt", "head")
    prompt_count = lax.axis_size("prompt")
    rows_here, head_dim = queries.shape
    half_feat = states.shape[1]
    column_count = states.shape[2] // 2
    heads_held = column_count // head_dim
    groups = prompt_count * KVH
    capacity = 2 * rows_here // groups
    slots = groups * capacity
    cols = slots // heads_held // LANES
    units = heads_held * cols
    vmem = pl.BlockSpec(memory_space=pltpu.VMEM)
    hbm = pl.BlockSpec(memory_space=pltpu.HBM)
    params = pltpu.CompilerParams(vmem_limit_bytes=48 * 1024 * 1024)
    route = row_route.reshape(1, rows_here)
    live = row_live.reshape(1, rows_here)
    inputs = [
        pltpu.with_memory_space_constraint(array, pltpu.HBM)
        for array in (route, live, queries, out_grad, states[0])
    ]
    send, held = pl.pallas_call(
        functools.partial(pack_kernel, capacity),
        out_shape=(
            pltpu.VMEM((slots, 2 * head_dim), jnp.bfloat16),
            pltpu.VMEM((half_feat // 2, 2 * head_dim), jnp.bfloat16),
        ),
        in_specs=[hbm] * 5,
        out_specs=(vmem, vmem),
        scratch_shapes=[
            pltpu.VMEM((1, rows_here), jnp.int32),
            pltpu.VMEM((1, rows_here), jnp.int32),
            pltpu.VMEM((rows_here, 2 * head_dim), jnp.bfloat16),
            pltpu.VMEM((rows_here, rows_here), jnp.bfloat16),
            pltpu.SemaphoreType.DMA((5,)),
        ],
        compiler_params=pltpu.CompilerParams(vmem_limit_bytes=16 * 1024 * 1024),
        name="pack_rows",
    )(*inputs)
    recv = lax.all_to_all(send, axes, split_axis=0, concat_axis=0, tiled=True)
    recv = pltpu.with_memory_space_constraint(recv, pltpu.VMEM)
    answer = pl.pallas_call(
        functools.partial(query_kernel, heads_held, capacity),
        out_shape=jax.ShapeDtypeStruct((slots, head_dim), jnp.bfloat16),
        in_specs=[vmem, vmem, hbm],
        out_specs=vmem,
        scratch_shapes=[
            pltpu.VMEM((half_feat - half_feat // 2, 2 * head_dim), jnp.bfloat16),
            pltpu.VMEM((max(heads_held - 1, 1), half_feat, 2 * head_dim), jnp.bfloat16),
            pltpu.VMEM((units, head_dim, LANES), jnp.float32),
            pltpu.VMEM((2 * heads_held, 2 * head_dim, slots // heads_held), jnp.bfloat16),
            pltpu.VMEM((2, cols, half_feat, LANES), jnp.float32),
            pltpu.VMEM((2, cols, half_feat, LANES), jnp.float32),
            pltpu.VMEM((cols, head_dim * SUB, LANES), jnp.float32),
            pltpu.VMEM((units, head_dim, LANES), jnp.float32),
            pltpu.SemaphoreType.DMA((heads_held,)),
        ],
        compiler_params=pltpu.CompilerParams(vmem_limit_bytes=48 * 1024 * 1024),
        name="query_side",
    )(held, recv, inputs[4])
    back = lax.all_to_all(answer, axes, split_axis=0, concat_axis=0, tiled=True)
    back = pltpu.with_memory_space_constraint(back, pltpu.VMEM)
    state_grad, pick = pl.pallas_call(
        functools.partial(state_kernel, heads_held, capacity),
        out_shape=(
            jax.ShapeDtypeStruct((half_feat, 2 * column_count), jnp.float32),
            pltpu.VMEM((rows_here, slots), jnp.bfloat16),
        ),
        in_specs=[vmem, vmem],
        out_specs=(hbm, vmem),
        scratch_shapes=[
            pltpu.VMEM((units, head_dim, LANES), jnp.float32),
            pltpu.VMEM((2 * heads_held, slots // heads_held, 2 * head_dim), jnp.bfloat16),
            pltpu.VMEM((cols, 2, half_feat, LANES), jnp.float32),
            pltpu.VMEM((cols, 2, half_feat, LANES), jnp.float32),
            pltpu.VMEM((heads_held, half_feat, 2 * head_dim), jnp.float32),
            pltpu.SemaphoreType.DMA((heads_held, cols)),
        ],
        compiler_params=params,
        name="state_side",
    )(recv, route)
    pick = pltpu.with_memory_space_constraint(pick, pltpu.VMEM)
    query_grad = pl.pallas_call(
        unpack_kernel,
        out_shape=jax.ShapeDtypeStruct((rows_here, head_dim), jnp.bfloat16),
        in_specs=[vmem] * 2,
        out_specs=vmem,
        name="unpack_rows",
    )(pick, back)
    return (query_grad, state_grad[None])


def whole_heads(queries, states):
    rows_here, head_dim = queries.shape
    groups = lax.axis_size("prompt") * KVH
    capacity = 2 * rows_here // groups
    column_count = states.shape[2] // 2
    heads_held = column_count // head_dim
    return (
        head_dim == LANES
        and heads_held >= 1
        and column_count % head_dim == 0
        and capacity % SUB == 0
        and groups * capacity // heads_held == 2 * LANES
        and states.shape[1] % (2 * SUB * (groups * capacity // heads_held // LANES)) == 0
    )


def per_device(*arrays):
    if whole_heads(arrays[0], arrays[4]):
        return fast_device(*arrays)
    return general_device(*arrays)


def solution(mesh):
    return jax.shard_map(
        per_device,
        mesh=mesh,
        in_specs=(
            P(("prompt", "head"), None),
            P(("prompt", "head"), None),
            P(("prompt", "head"), None),
            P(("prompt", "head")),
            P("prompt", None, "head"),
        ),
        out_specs=(P(("prompt", "head"), None), P("prompt", None, "head")),
        check_vma=False,
    )
```

```python
import functools

import jax
import jax.numpy as jnp
import numpy as np
from jax import lax
from jax.experimental import pallas as pl
from jax.experimental.pallas import tpu as pltpu
from jax.sharding import PartitionSpec as P

KVH = 32


def score_grads(query_rows, grad_rows, sym_block, diag_block, mask_table):
    row_count, head_dim = query_rows.shape
    col_width = grad_rows.shape[1]
    block_rows = min(256, row_count)
    root_two = float(np.sqrt(2.0))
    query_blocks = query_rows.reshape(row_count // block_rows, block_rows, head_dim)
    grad_blocks = grad_rows.reshape(row_count // block_rows, block_rows, col_width)
    diag_float = diag_block.astype(jnp.float32)

    def block_step(total_grad, pair):
        query_block, grad_block = pair
        query_float = query_block.astype(jnp.float32)
        square = query_float[:, :, None] * query_float[:, None, :] * mask_table
        stored = square.reshape(block_rows, head_dim * head_dim).astype(jnp.bfloat16)
        total_grad = total_grad + lax.dot_general(
            stored, grad_block, (((0,), (0,)), ((), ())), preferred_element_type=jnp.float32
        )
        sweep = jnp.dot(query_block, sym_block, preferred_element_type=jnp.float32).reshape(
            block_rows, head_dim, col_width
        )
        sweep = (
            root_two * sweep
            - (2.0 * root_two - 2.0) * query_float[:, :, None] * diag_float[None, :, :]
        )
        grad_float = grad_block.astype(jnp.float32)
        query_part = jnp.einsum("baj,bj->ba", sweep, grad_float, precision=lax.Precision.HIGHEST)
        return (total_grad, query_part)

    start_grad = jnp.zeros((head_dim * head_dim, col_width), jnp.float32)
    total_grad, query_parts = lax.scan(block_step, start_grad, (query_blocks, grad_blocks))
    return (query_parts.reshape(row_count, head_dim), total_grad)


def general_device(queries, out_grad, row_route, row_live, states):
    prompt_count = lax.axis_size("prompt")
    head_count = lax.axis_size("head")
    rows_here, head_dim = queries.shape
    half_feat = states.shape[1]
    feat_count = 2 * half_feat
    column_count = states.shape[2] // 2
    kv_heads = KVH
    col_width = min(column_count, head_dim)
    copies = head_dim // col_width
    heads_held = column_count // col_width
    groups = prompt_count * kv_heads
    capacity = 2 * rows_here // groups
    first_index, second_index = np.triu_indices(head_dim)
    dense_place = (first_index * head_dim + second_index).astype(np.int32)
    triangle_of = np.full(head_dim * head_dim, feat_count, np.int32)
    triangle_of[dense_place] = np.arange(feat_count, dtype=np.int32)
    diagonal_of = triangle_of[np.arange(head_dim) * head_dim + np.arange(head_dim)]
    mask_np = np.zeros((head_dim, head_dim), np.float32)
    mask_np[first_index, second_index] = np.where(first_index == second_index, 1.0, np.sqrt(2.0))
    mask_table = jnp.asarray(mask_np)
    route_ids = row_route[:, 0]
    one_hot = (route_ids[:, None] == jnp.arange(groups, dtype=jnp.int32)[None, :]).astype(jnp.int32)
    slot_rank = jnp.sum(jnp.cumsum(one_hot, axis=0) * one_hot, axis=1) - 1
    slot_place = route_ids * capacity + slot_rank
    live_mask = row_live.astype(jnp.float32)[:, None]
    query_live = (queries.astype(jnp.float32) * live_mask).astype(jnp.bfloat16)
    grad_live = (out_grad.astype(jnp.float32) * live_mask).astype(jnp.bfloat16)
    query_bucket = (
        jnp.zeros((groups * capacity, head_dim), jnp.bfloat16).at[slot_place].set(query_live)
    )
    grad_bucket = (
        jnp.zeros((groups * capacity, head_dim), jnp.bfloat16).at[slot_place].set(grad_live)
    )
    query_send = jnp.broadcast_to(
        query_bucket.reshape(prompt_count, kv_heads, 1, capacity, head_dim),
        (prompt_count, kv_heads, copies, capacity, head_dim),
    )
    query_send = query_send.reshape(prompt_count, head_count, heads_held * capacity, head_dim)
    grad_send = grad_bucket.reshape(prompt_count, kv_heads, capacity, copies, col_width).transpose(
        0, 1, 3, 2, 4
    )
    grad_send = grad_send.reshape(prompt_count, head_count, heads_held * capacity, col_width)
    sectioned_query, sectioned_grad = (
        lax.all_to_all(query_send, "head", split_axis=1, concat_axis=1, tiled=True),
        lax.all_to_all(grad_send, "head", split_axis=1, concat_axis=1, tiled=True),
    )
    query_recv, grad_recv = (
        lax.all_to_all(sectioned_query, "prompt", split_axis=0, concat_axis=0, tiled=True),
        lax.all_to_all(sectioned_grad, "prompt", split_axis=0, concat_axis=0, tiled=True),
    )
    query_items = query_recv.reshape(prompt_count * head_count, heads_held, capacity, head_dim)
    grad_items = grad_recv.reshape(prompt_count * head_count, heads_held, capacity, col_width)
    local_state = (
        states[0]
        .reshape(half_feat, column_count, 2)
        .transpose(0, 2, 1)
        .reshape(feat_count, column_count)
    )
    padded_state = jnp.concatenate(
        [local_state, jnp.zeros((1, column_count), local_state.dtype)], axis=0
    )
    upper_state = padded_state[triangle_of].reshape(head_dim, head_dim, column_count)
    sym_state = upper_state + jnp.swapaxes(upper_state, 0, 1)
    diag_state = local_state[diagonal_of]
    query_shares = []
    state_shares = []
    for index in range(heads_held):
        query_rows = query_items[:, index].reshape(-1, head_dim)
        grad_rows = grad_items[:, index].reshape(-1, col_width)
        sym_block = sym_state[:, :, index * col_width : (index + 1) * col_width].reshape(
            head_dim, head_dim * col_width
        )
        diag_block = diag_state[:, index * col_width : (index + 1) * col_width]
        query_part, dense_grad = score_grads(
            query_rows, grad_rows, sym_block, diag_block, mask_table
        )
        query_shares.append(query_part.reshape(prompt_count * head_count, capacity, head_dim))
        state_shares.append(dense_grad[dense_place])
    query_partial = jnp.stack(query_shares, axis=1).reshape(
        prompt_count, head_count, heads_held * capacity, head_dim
    )
    state_full = jnp.concatenate(state_shares, axis=1)
    state_grad = (
        state_full.reshape(half_feat, 2, column_count)
        .transpose(0, 2, 1)
        .reshape(1, half_feat, 2 * column_count)
    )
    halfway = lax.all_to_all(query_partial, "head", split_axis=1, concat_axis=1, tiled=True)
    returned = lax.all_to_all(halfway, "prompt", split_axis=0, concat_axis=0, tiled=True)
    query_total = jnp.sum(
        returned.reshape(prompt_count, kv_heads, copies, capacity, head_dim), axis=2
    )
    query_grad = query_total.reshape(groups * capacity, head_dim)[slot_place].astype(jnp.bfloat16)
    return (query_grad, state_grad)


LANES = 128
SUB = 8


def pair_runs(head_dim):
    runs = []
    for a in range(head_dim):
        offset = a * head_dim - a * (a - 1) // 2
        for parity in range(2):
            b = a + (parity - offset) % 2
            if b < head_dim:
                first = (offset + b - a - parity) // 2
                runs.append((a, parity, b & 1, b >> 1, first, b == a))
    return runs


def split_place(index, head_dim):
    return (index & 1) * (head_dim // 2) + (index >> 1)


def eye_of(size):
    return (
        lax.broadcasted_iota(jnp.int32, (size, size), 0)
        == lax.broadcasted_iota(jnp.int32, (size, size), 1)
    )


def parity_split(size):
    row = lax.broadcasted_iota(jnp.int32, (size, size), 0)
    col = lax.broadcasted_iota(jnp.int32, (size, size), 1)
    half = size // 2
    wanted = jnp.where(row < half, 2 * row, 2 * (row - half) + 1)
    return (col == wanted).astype(jnp.bfloat16)


def triangle(rows):
    first = lax.broadcasted_iota(jnp.int32, (rows, rows), 0)
    second = lax.broadcasted_iota(jnp.int32, (rows, rows), 1)
    return (first < second).astype(jnp.float32).astype(jnp.bfloat16)


def slot_row(route, earlier, groups, capacity):
    rows = route.shape[1]
    named = lax.broadcasted_iota(jnp.int32, (groups, rows), 0) == route
    named = named.astype(jnp.float32)
    before = jnp.dot(named.astype(jnp.bfloat16), earlier, preferred_element_type=jnp.float32)
    rank = jnp.sum(named * before, axis=0, keepdims=True)
    return route.astype(jnp.float32) * capacity + rank


def pack_kernel(
    capacity, route_hbm, live_hbm, query_hbm, grad_hbm, states_hbm,
    send_ref, held_ref, route_ref, live_ref, pair_ref, earlier_ref, sem,
):
    rows, head_dim = query_hbm.shape
    slots = send_ref.shape[0]
    pairs = [
        (route_hbm, route_ref),
        (live_hbm, live_ref),
        (query_hbm, pair_ref.at[:, pl.ds(0, head_dim)]),
        (grad_hbm, pair_ref.at[:, pl.ds(head_dim, head_dim)]),
        (states_hbm.at[pl.ds(0, held_ref.shape[0]), pl.ds(0, held_ref.shape[1])], held_ref),
    ]
    copies = [pltpu.make_async_copy(*pair, sem.at[i]) for i, pair in enumerate(pairs)]
    for copy in copies:
        copy.start()
    earlier_ref[...] = triangle(rows)
    for copy in copies[:4]:
        copy.wait()
    place = slot_row(route_ref[...], earlier_ref[...], slots // capacity, capacity)
    place = jnp.where(live_ref[...] != 0, place.astype(jnp.int32), -1)
    pick = lax.broadcasted_iota(jnp.int32, (slots, rows), 0) == place
    pick = pick.astype(jnp.float32).astype(jnp.bfloat16)
    send_ref[...] = jnp.dot(
        pick, pair_ref[...], preferred_element_type=jnp.float32
    ).astype(jnp.bfloat16)
    copies[4].wait()


def unpack_kernel(pick_ref, back_ref, out_ref):
    out_ref[...] = jnp.dot(
        pick_ref[...], back_ref[...], preferred_element_type=jnp.float32
    ).astype(jnp.bfloat16)


def head_rows(recv_ref, head, heads_held, capacity):
    slots, width = recv_ref.shape
    whole = recv_ref[...].astype(jnp.float32)
    split = whole.reshape(slots // (heads_held * capacity), heads_held, capacity, width)
    return split[:, head].reshape(slots // heads_held, width).astype(jnp.bfloat16)


def stuff_transposed(grad, parity):
    width = grad.shape[1]
    row = lax.broadcasted_iota(jnp.int32, (2 * width, width), 0)
    col = lax.broadcasted_iota(jnp.int32, (2 * width, width), 1)
    place = (row == 2 * col + parity).astype(jnp.bfloat16)
    return lax.dot_general(
        place, grad, (((1,), (1,)), ((), ())), preferred_element_type=jnp.float32
    ).astype(jnp.bfloat16)


def stuff(grad, parity):
    width = grad.shape[1]
    row = lax.broadcasted_iota(jnp.int32, (width, 2 * width), 0)
    col = lax.broadcasted_iota(jnp.int32, (width, 2 * width), 1)
    place = (col == 2 * row + parity).astype(jnp.bfloat16)
    return jnp.dot(grad, place, preferred_element_type=jnp.float32).astype(jnp.bfloat16)


def split_query(query):
    return lax.dot_general(
        parity_split(query.shape[1]),
        query,
        (((1,), (1,)), ((), ())),
        preferred_element_type=jnp.float32,
    )


def run_weight(start, diagonal, on_diagonal, off_diagonal):
    row = lax.broadcasted_iota(jnp.int32, (SUB, LANES), 0)
    value = jnp.where(row >= start, jnp.float32(off_diagonal), jnp.float32(0.0))
    if diagonal:
        value = jnp.where(row == start, jnp.float32(on_diagonal), value)
    return value


def load_split(xt_ref, t, head_dim):
    half = head_dim // 2
    return [
        [xt_ref[t, at : at + SUB, :] for at in range(side * half, (side + 1) * half, SUB)]
        for side in range(2)
    ]


def prepare(recv_ref, xt_ref, heads_held, capacity):
    slots, width = recv_ref.shape
    head_dim = width // 2
    cols = slots // heads_held // LANES
    grads = []
    for head in range(heads_held):
        block = head_rows(recv_ref, head, heads_held, capacity)
        grads.append(block[:, head_dim:])
        turned = split_query(block[:, :head_dim])
        for col in range(cols):
            xt_ref[head * cols + col] = turned[:, col * LANES : (col + 1) * LANES]
    return grads


def query_kernel(
    heads_held, capacity, held_ref, recv_ref, states_hbm, out_ref,
    late_ref, rest_ref, xt_ref, stuffed_ref, even_ref, odd_ref, acc_ref, dqt_ref, stage_ref, sem, out_sem,
):
    half_feat, lanes = states_hbm.shape
    early = held_ref.shape[0]
    slots, width = recv_ref.shape
    head_dim = width // 2
    half = head_dim // 2
    wide = lanes // heads_held
    rows = slots // heads_held
    cols = rows // LANES
    regs = half // SUB
    runs = pair_runs(head_dim)
    inv_root = float(np.sqrt(0.5))
    root = float(np.sqrt(2.0))
    feat_refs = [even_ref, odd_ref]

    def fetch(head):
        if head == 0:
            source, target = states_hbm.at[pl.ds(early, half_feat - early), pl.ds(0, wide)], late_ref
        else:
            source, target = states_hbm.at[:, pl.ds(head * wide, wide)], rest_ref.at[head - 1]
        return pltpu.make_async_copy(source, target, sem.at[head])

    for head in range(heads_held):
        fetch(head).start()
    grads = prepare(recv_ref, xt_ref, heads_held, capacity)
    for head in range(heads_held):
        for parity in range(2):
            stuffed_ref[2 * head + parity] = stuff_transposed(grads[head], parity)

    def expand(head, parity, start, stop):
        rows_of = pl.ds(start, stop - start)
        if head > 0:
            block = rest_ref[head - 1, rows_of]
        elif stop <= early:
            block = held_ref[rows_of]
        else:
            if start == early and parity == 0:
                fetch(0).wait()
            block = late_ref[start - early : stop - early]
        feat = jnp.dot(block, stuffed_ref[2 * head + parity], preferred_element_type=jnp.float32)
        for col in range(cols):
            feat_refs[head % 2][parity, col, rows_of] = feat[:, col * LANES : (col + 1) * LANES]

    parts = 2
    tile = 2 * SUB
    bounds = [half_feat * i // parts // tile * tile for i in range(parts)] + [half_feat]
    middle = next(a for a in range(head_dim) if a * head_dim - a * (a - 1) // 2 >= half_feat) - 1
    spans = [(0, middle), (middle, head_dim)]

    def reduce(head, col, part):
        low, high = spans[part]
        feat_ref = feat_refs[head % 2]
        t = head * cols + col
        values = load_split(xt_ref, t, head_dim)
        if part == 0:
            totals = [[None] * regs for _ in range(2)]
        else:
            totals = load_split(dqt_ref, t, head_dim)
        for a in range(low, high):
            at = split_place(a, head_dim)
            own = jnp.broadcast_to(xt_ref[t, at : at + 1, :], (SUB, LANES))
            acc = None
            for owner, parity, side, start, first, diagonal in runs:
                if owner != a:
                    continue
                for m in range(start // SUB, regs):
                    place = first - start + m * SUB
                    feat = feat_ref[parity, col, place : place + SUB, :]
                    if m == start // SUB and (start % SUB or diagonal):
                        feat = feat * run_weight(start % SUB, diagonal, inv_root, 1.0)
                    term = feat * values[side][m]
                    acc = term if acc is None else acc + term
                    other = feat * own
                    totals[side][m] = other if totals[side][m] is None else totals[side][m] + other
            acc_ref[col, at * SUB : (at + 1) * SUB, :] = acc
        for side in range(2):
            for m in range(regs):
                at = side * half + m * SUB
                total = totals[side][m]
                if part == 1:
                    for k in range(SUB):
                        total = total + acc_ref[col, pl.ds(at * SUB + k, SUB, stride=SUB), :]
                    total = total * root
                dqt_ref[t, at : at + SUB, :] = total

    back = parity_split(head_dim)
    span = slots // cols

    def deliver(col):
        return pltpu.make_async_copy(
            stage_ref.at[pl.ds(col * span, span)], out_ref.at[pl.ds(col * span, span)], out_sem.at[col]
        )

    def finish(col):
        pieces = []
        for head in range(heads_held):
            part = lax.dot_general(
                dqt_ref[head * cols + col].astype(jnp.bfloat16),
                back,
                (((0,), (0,)), ((), ())),
                preferred_element_type=jnp.float32,
            )
            pieces.append(part.reshape(LANES // capacity, 1, capacity, head_dim))
        joined = jnp.concatenate(pieces, axis=1).reshape(span, head_dim)
        stage_ref[col * span : (col + 1) * span, :] = joined.astype(stage_ref.dtype)

    regions = [([(0, 0)], [(0, 0, 0)]), ([(0, 1)], [(0, 1, 0), (0, 0, 1)])]
    for head in range(1, heads_held):
        regions.append(([(head, 0)], [(head - 1, 1, 1), (head, 0, 0)]))
        regions.append(([(head, 1)], [(head, 1, 0), (head, 0, 1)]))
    regions.append(([], [(heads_held - 1, 1, 1)]))

    def step(now, carry):
        for number, (ahead, segments) in enumerate(regions):

            @pl.when(now == number)
            def _():
                for head, group in ahead:
                    if head > 0 and group == 0:
                        fetch(head).wait()
                    for i in range(group * parts // 2, (group + 1) * parts // 2):
                        for parity in range(2):
                            expand(head, parity, bounds[i], bounds[i + 1])
                if not ahead:
                    for col in range(cols - 1):
                        finish(col)
                for head, col, part in segments:
                    reduce(head, col, part)
                if not ahead:
                    for col in range(cols - 1):
                        deliver(col).start()

        return carry

    lax.fori_loop(0, len(regions), step, 0)
    finish(cols - 1)
    deliver(cols - 1).start()
    for col in range(cols):
        deliver(col).wait()


def state_kernel(
    heads_held, capacity, recv_ref, route_ref, out_ref, pick_ref,
    xt_ref, stuffed_ref, first_ref, second_ref, out_buf, sem,
):
    half_feat, lanes = out_ref.shape
    slots, width = recv_ref.shape
    head_dim = width // 2
    wide = lanes // heads_held
    rows = slots // heads_held
    cols = rows // LANES
    piece = half_feat // cols
    runs = pair_runs(head_dim)
    regs = head_dim // 2 // SUB
    root = float(np.sqrt(2.0))
    feat_refs = [first_ref, second_ref]
    grads = prepare(recv_ref, xt_ref, heads_held, capacity)
    for head in range(heads_held):
        for parity in range(2):
            stuffed_ref[2 * head + parity] = stuff(grads[head], parity)

    def store_of(head, col):
        at = pl.multiple_of(col * piece, SUB)
        return pltpu.make_async_copy(
            out_buf.at[head, pl.ds(at, piece)],
            out_ref.at[pl.ds(at, piece), pl.ds(head * wide, wide)],
            sem.at[head, col],
        )

    def expand(head, col):
        feat_ref = feat_refs[head % 2]
        t = head * cols + col
        values = load_split(xt_ref, t, head_dim)
        for a, parity, side, start, first, diagonal in reversed(runs):
            at = split_place(a, head_dim)
            own = jnp.broadcast_to(xt_ref[t, at : at + 1, :], (SUB, LANES))
            for m in range(start // SUB, regs):
                place = first - start + m * SUB
                value = values[side][m] * own
                if diagonal and m == start // SUB:
                    value = value * run_weight(start % SUB, True, 1.0, root)
                else:
                    value = value * root
                feat_ref[col, parity, place : place + SUB, :] = value

    def product(head, col):
        feat_ref = feat_refs[head % 2]
        at = pl.multiple_of(col * piece, SUB)
        total = None
        for parity in range(2):
            part = jnp.concatenate(
                [feat_ref[other, parity, pl.ds(at, piece), :].astype(jnp.bfloat16) for other in range(cols)],
                axis=1,
            )
            term = jnp.dot(part, stuffed_ref[2 * head + parity], preferred_element_type=jnp.float32)
            total = term if total is None else total + term
        out_buf[head, pl.ds(at, piece), :] = total

    for head in range(heads_held + 1):

        def step(col, carry):
            if head > 0:
                product(head - 1, col)
            if head < heads_held:
                expand(head, col)
            if head > 0:
                store_of(head - 1, col).start()
            return carry

        lax.fori_loop(0, cols, step, 0)

    here = route_ref.shape[1]
    place = slot_row(route_ref[...], triangle(here), slots // capacity, capacity)
    column = jnp.sum(
        jnp.where(eye_of(here), jnp.broadcast_to(place, (here, here)), 0.0), axis=1, keepdims=True
    )
    pick = lax.broadcasted_iota(jnp.int32, (here, slots), 1) == column.astype(jnp.int32)
    pick_ref[...] = pick.astype(jnp.float32).astype(jnp.bfloat16)

    def drain(col, carry):
        for head in range(heads_held):
            store_of(head, col).wait()
        return carry

    lax.fori_loop(0, cols, drain, 0)


def fast_device(queries, out_grad, row_route, row_live, states):
    axes = ("prompt", "head")
    prompt_count = lax.axis_size("prompt")
    rows_here, head_dim = queries.shape
    half_feat = states.shape[1]
    column_count = states.shape[2] // 2
    heads_held = column_count // head_dim
    groups = prompt_count * KVH
    capacity = 2 * rows_here // groups
    slots = groups * capacity
    cols = slots // heads_held // LANES
    units = heads_held * cols
    vmem = pl.BlockSpec(memory_space=pltpu.VMEM)
    hbm = pl.BlockSpec(memory_space=pltpu.HBM)
    params = pltpu.CompilerParams(vmem_limit_bytes=48 * 1024 * 1024)
    route = row_route.reshape(1, rows_here)
    live = row_live.reshape(1, rows_here)
    inputs = [
        pltpu.with_memory_space_constraint(array, pltpu.HBM)
        for array in (route, live, queries, out_grad, states[0])
    ]
    send, held = pl.pallas_call(
        functools.partial(pack_kernel, capacity),
        out_shape=(
            pltpu.VMEM((slots, 2 * head_dim), jnp.bfloat16),
            pltpu.VMEM((half_feat // 2, 2 * head_dim), jnp.bfloat16),
        ),
        in_specs=[hbm] * 5,
        out_specs=(vmem, vmem),
        scratch_shapes=[
            pltpu.VMEM((1, rows_here), jnp.int32),
            pltpu.VMEM((1, rows_here), jnp.int32),
            pltpu.VMEM((rows_here, 2 * head_dim), jnp.bfloat16),
            pltpu.VMEM((rows_here, rows_here), jnp.bfloat16),
            pltpu.SemaphoreType.DMA((5,)),
        ],
        compiler_params=pltpu.CompilerParams(vmem_limit_bytes=16 * 1024 * 1024),
        name="pack_rows",
    )(*inputs)
    recv = lax.all_to_all(send, axes, split_axis=0, concat_axis=0, tiled=True)
    recv = pltpu.with_memory_space_constraint(recv, pltpu.VMEM)
    answer = pl.pallas_call(
        functools.partial(query_kernel, heads_held, capacity),
        out_shape=jax.ShapeDtypeStruct((slots, head_dim), jnp.bfloat16),
        in_specs=[vmem, vmem, hbm],
        out_specs=vmem,
        scratch_shapes=[
            pltpu.VMEM((half_feat - half_feat // 2, 2 * head_dim), jnp.bfloat16),
            pltpu.VMEM((max(heads_held - 1, 1), half_feat, 2 * head_dim), jnp.bfloat16),
            pltpu.VMEM((units, head_dim, LANES), jnp.float32),
            pltpu.VMEM((2 * heads_held, 2 * head_dim, slots // heads_held), jnp.bfloat16),
            pltpu.VMEM((2, cols, half_feat, LANES), jnp.float32),
            pltpu.VMEM((2, cols, half_feat, LANES), jnp.float32),
            pltpu.VMEM((cols, head_dim * SUB, LANES), jnp.float32),
            pltpu.VMEM((units, head_dim, LANES), jnp.float32),
            pltpu.VMEM((slots, head_dim), jnp.bfloat16),
            pltpu.SemaphoreType.DMA((heads_held,)),
            pltpu.SemaphoreType.DMA((cols,)),
        ],
        compiler_params=pltpu.CompilerParams(vmem_limit_bytes=48 * 1024 * 1024),
        name="query_side",
    )(held, recv, inputs[4])
    back = lax.all_to_all(answer, axes, split_axis=0, concat_axis=0, tiled=True)
    back = pltpu.with_memory_space_constraint(back, pltpu.VMEM)
    state_grad, pick = pl.pallas_call(
        functools.partial(state_kernel, heads_held, capacity),
        out_shape=(
            jax.ShapeDtypeStruct((half_feat, 2 * column_count), jnp.float32),
            pltpu.VMEM((rows_here, slots), jnp.bfloat16),
        ),
        in_specs=[vmem, vmem],
        out_specs=(hbm, vmem),
        scratch_shapes=[
            pltpu.VMEM((units, head_dim, LANES), jnp.float32),
            pltpu.VMEM((2 * heads_held, slots // heads_held, 2 * head_dim), jnp.bfloat16),
            pltpu.VMEM((cols, 2, half_feat, LANES), jnp.float32),
            pltpu.VMEM((cols, 2, half_feat, LANES), jnp.float32),
            pltpu.VMEM((heads_held, half_feat, 2 * head_dim), jnp.float32),
            pltpu.SemaphoreType.DMA((heads_held, cols)),
        ],
        compiler_params=params,
        name="state_side",
    )(recv, route)
    pick = pltpu.with_memory_space_constraint(pick, pltpu.VMEM)
    query_grad = pl.pallas_call(
        unpack_kernel,
        out_shape=jax.ShapeDtypeStruct((rows_here, head_dim), jnp.bfloat16),
        in_specs=[vmem] * 2,
        out_specs=vmem,
        name="unpack_rows",
    )(pick, back)
    return (query_grad, state_grad[None])


def whole_heads(queries, states):
    rows_here, head_dim = queries.shape
    groups = lax.axis_size("prompt") * KVH
    capacity = 2 * rows_here // groups
    column_count = states.shape[2] // 2
    heads_held = column_count // head_dim
    return (
        head_dim == LANES
        and heads_held >= 1
        and column_count % head_dim == 0
        and capacity % SUB == 0
        and groups * capacity // heads_held == 2 * LANES
        and states.shape[1] % (2 * SUB * (groups * capacity // heads_held // LANES)) == 0
    )


def per_device(*arrays):
    if whole_heads(arrays[0], arrays[4]):
        return fast_device(*arrays)
    return general_device(*arrays)


def solution(mesh):
    return jax.shard_map(
        per_device,
        mesh=mesh,
        in_specs=(
            P(("prompt", "head"), None),
            P(("prompt", "head"), None),
            P(("prompt", "head"), None),
            P(("prompt", "head")),
            P("prompt", None, "head"),
        ),
        out_specs=(P(("prompt", "head"), None), P("prompt", None, "head")),
        check_vma=False,
    )
```
